256 devices in a mesh: tx: 16 (over z, core), ty: 8 (over x_hi, y), mode: 2 (over x_lo).
Axes of the slice: x: 4 (x_hi: 2, x_lo: 2; x = x_hi * 2 + x_lo), y: 4, z: 8, core: 2. Of those that a mesh axis runs over, the one named last changes fastest.
Arguments:
- obj: float32 [2, 4096, 8192], P(None, 'tx', 'ty'), may hold values from -4 to 4
- probe: float32 [4, 2, 256, 256], P('mode'), may hold values from -4 to 4
- intensity: float32 [16, 8, 2, 256, 256], P('tx', 'ty'), may hold values from 0 to 2
- offsets: int32 [16, 8, 2, 2], P('tx', 'ty'), may hold values from 0 to 1023, as said below
- counts: int32 [16, 8], P('tx', 'ty'), may hold values from 1 to 2, as said below
- patch_filters: float32 [16, 4], replicated, may hold values from -2 to 2
Outputs:
- new_obj: float32 [2, 4096, 8192], P(None, 'tx', 'ty')
The draws below stay inside these ranges and needn't reach their ends.
Inputs may be any that keep to these rules, and one draw needn't show every extreme that they name: Row offsets are below 256, column offsets below 1024; a pattern may reach into the tiles below and to the right. Slots from counts[a,b] on are empty.
All inputs are finite; a program needn't handle non-finite values.
Results may differ from the reference program's by a relative error of at most 0.00012.
Values sent between devices are 32-bit elements; how exact they have to be, the bound alone decides.
No kernel may reach another device: no remote copies, remote signals or barrier semaphores. Data moves between devices by JAX's collectives and lax.ppermute only.
A program may use at most 128 MiB of HBM per device.

```python
import math
import jax
import jax.numpy as jnp
from jax import lax

P_SIZE = 256
MODES = 4
FILT = 16
TH = 256
TW = 1024
CAP = 2
NH = 4096
NW = 8192
N_TX = 16
N_TY = 8


def draw_offsets(key, part):
    key_rows, key_cols, key_pick, key_other = jax.random.split(jax.random.fold_in(key, 11), 4)
    tiles = N_TX * N_TY
    rows = jax.random.randint(key_rows, (tiles, CAP), 0, TH)
    cols = jax.random.randint(key_cols, (tiles, CAP), 0, TW)
    rows = rows.at[jax.random.randint(key_pick, (), 0, tiles), 0].set(TH - 1)
    cols = cols.at[jax.random.randint(key_other, (), 0, tiles), 0].set(TW - 1)
    stacked = jnp.stack([rows, cols], axis=-1)
    return stacked.reshape(N_TX, N_TY, CAP, 2).astype(jnp.int32)


def draw_counts(key, part):
    key_counts, key_pick = jax.random.split(jax.random.fold_in(key, 23), 2)
    tiles = N_TX * N_TY
    counts = jax.random.randint(key_counts, (tiles,), CAP // 2, CAP + 1)
    counts = counts.at[jax.random.randint(key_pick, (), 0, tiles)].set(CAP)
    return counts.reshape(N_TX, N_TY).astype(jnp.int32)


def level_of(key, dims, shards, smallest, high):
    def one(position, shards_of):
        draws = jax.random.uniform(jax.random.fold_in(jax.random.fold_in(key, 6), position), (shards_of,), jnp.float32, smallest / len(shards), high / len(shards))
        return jnp.repeat(jnp.exp(draws), dims[position] // shards_of).reshape((-1,) + (1,) * (len(dims) - position - 1))

    loudness = one(*shards[0])
    for cut in shards[1:]:
        loudness = loudness * one(*cut)
    return loudness


def bell_draw(key, shape, spread, most, cuts=(), held_as=jnp.bfloat16):
    level = level_of(key, shape, cuts, -0.22, 0.18) if cuts else 1.0
    entries = jax.random.normal(key, shape, jnp.float32) * spread * level
    return jnp.minimum(jnp.maximum(entries, -most), most).astype(held_as)


def setup_inputs(seed: int = 0) -> dict:
    key_of = jax.random.split(jax.random.key(seed), 7)
    obj = bell_draw(key_of[0], (2, NH, NW), 0.5, 4.0, ((1, 16), (2, 8)), jnp.float32)
    probe = bell_draw(key_of[1], (MODES, 2, P_SIZE, P_SIZE), 0.5, 4.0, ((0, 2),), jnp.float32)
    intensity = jnp.clip(2.0 * jax.random.uniform(key_of[2], (N_TX, N_TY, CAP, P_SIZE, P_SIZE), jnp.float32) ** level_of(key_of[2], (N_TX, N_TY, CAP, P_SIZE, P_SIZE), ((0, 16), (1, 8)), -0.2, 0.2), 0.0, 2.0)
    offsets = draw_offsets(jax.random.fold_in(key_of[6], 71), 0)
    counts = draw_counts(jax.random.fold_in(key_of[6], 71), 0)
    patch_filters = bell_draw(key_of[5], (FILT, 4), 0.25, 2.0, (), jnp.float32)
    return {"obj": obj, "probe": probe, "intensity": intensity, "offsets": offsets, "counts": counts, "patch_filters": patch_filters}


highest = lax.Precision.HIGHEST
step_size = 0.25

def tables(length):
    ramp = jnp.arange(length, dtype=jnp.int32)
    product = ramp[:, None] * ramp[None, :] % length
    angle = product.astype(jnp.float32) * (2.0 * math.pi / length)
    scale = 1.0 / math.sqrt(length)
    return (jnp.cos(angle) * scale, -jnp.sin(angle) * scale)

def transform(real_part, imag_part, cos_tab, sin_tab):
    first_re = jnp.einsum('...k,kl->...l', real_part, cos_tab, precision=highest) - jnp.einsum('...k,kl->...l', imag_part, sin_tab, precision=highest)
    first_im = jnp.einsum('...k,kl->...l', real_part, sin_tab, precision=highest) + jnp.einsum('...k,kl->...l', imag_part, cos_tab, precision=highest)
    second_re = jnp.einsum('jk,...kl->...jl', cos_tab, first_re, precision=highest) - jnp.einsum('jk,...kl->...jl', sin_tab, first_im, precision=highest)
    second_im = jnp.einsum('jk,...kl->...jl', cos_tab, first_im, precision=highest) + jnp.einsum('jk,...kl->...jl', sin_tab, first_re, precision=highest)
    return (second_re, second_im)

def slot_grads(patches, probe, measured, cos_tab, sin_tab):
    probe_re = probe[None, :, 0]
    probe_im = probe[None, :, 1]
    obj_re = patches[:, None, 0]
    obj_im = patches[:, None, 1]
    exit_re = probe_re * obj_re - probe_im * obj_im
    exit_im = probe_re * obj_im + probe_im * obj_re
    wave_re, wave_im = transform(exit_re, exit_im, cos_tab, sin_tab)
    power = lax.optimization_barrier(jnp.sum(wave_re * wave_re + wave_im * wave_im, axis=1))
    resid = (power - measured)[:, None]
    back_re, back_im = transform(resid * wave_re, resid * wave_im, cos_tab, -sin_tab)
    grad_re = lax.optimization_barrier(jnp.sum(probe_re * back_re + probe_im * back_im, axis=1))
    grad_im = lax.optimization_barrier(jnp.sum(probe_re * back_im - probe_im * back_re, axis=1))
    return jnp.stack([grad_re, grad_im], axis=1)

def prior_term(window, filters, rows, cols):
    gram = jnp.dot(filters.T, filters, precision=highest)
    corners = [window[:, :rows, :cols], window[:, :rows, 1:], window[:, 1:, :cols], window[:, 1:, 1:]]
    mixed = [gram[which, 0] * corners[0] + gram[which, 1] * corners[1] + gram[which, 2] * corners[2] + gram[which, 3] * corners[3] for which in range(4)]
    total = jnp.pad(mixed[0], ((0, 0), (0, 1), (0, 1))) + jnp.pad(mixed[1], ((0, 0), (0, 1), (1, 0)))
    return total + jnp.pad(mixed[2], ((0, 0), (1, 0), (0, 1))) + jnp.pad(mixed[3], ((0, 0), (1, 0), (1, 0)))

def reference(obj, probe, intensity, offsets, counts, patch_filters):
    rows, cols = (obj.shape[1], obj.shape[2])
    padded = jnp.pad(obj, ((0, 0), (0, P_SIZE), (0, P_SIZE)))
    cos_tab, sin_tab = tables(P_SIZE)
    slots = N_TX * N_TY * CAP
    measured = intensity.reshape(slots, P_SIZE, P_SIZE)
    flat_offsets = offsets.reshape(slots, 2).astype(jnp.int32)
    ramp = jnp.arange(slots, dtype=jnp.int32)
    tile_row = ramp // (N_TY * CAP)
    tile_col = ramp // CAP % N_TY
    live = (ramp % CAP < counts.reshape(-1)[ramp // CAP]).astype(jnp.float32)
    zero = jnp.zeros((), jnp.int32)

    def add_slot(index, accum):
        row0 = (tile_row[index] * TH + flat_offsets[index, 0]).astype(jnp.int32)
        col0 = (tile_col[index] * TW + flat_offsets[index, 1]).astype(jnp.int32)
        patch = lax.dynamic_slice(padded, (zero, row0, col0), (2, P_SIZE, P_SIZE))
        grad = slot_grads(patch[None], probe, measured[index][None], cos_tab, sin_tab)[0] * live[index]
        current = lax.dynamic_slice(accum, (zero, row0, col0), (2, P_SIZE, P_SIZE))
        return lax.dynamic_update_slice(accum, current + grad, (zero, row0, col0))
    accum = lax.fori_loop(0, slots, add_slot, jnp.zeros(padded.shape, jnp.float32))
    prior = prior_term(padded[:, :rows + 1, :cols + 1], patch_filters, rows, cols)
    total = accum[:, :rows + 1, :cols + 1] + prior
    return obj - step_size * total[:, :rows, :cols]
```

```python
import functools
import math

import jax
import jax.numpy as jnp
import numpy as np
from jax import lax
from jax.experimental import pallas as pl
from jax.experimental.pallas import tpu as pltpu
from jax.sharding import PartitionSpec as P


W = 256
axes = ("tx", "ty", "mode")
step_size = 0.25
f32 = jnp.float32
bf16 = jnp.bfloat16
VMEM = pl.BlockSpec(memory_space=pltpu.VMEM)
SMEM = pl.BlockSpec(memory_space=pltpu.SMEM)


def rings(mesh):
    n_tx, n_ty = mesh.shape["tx"], mesh.shape["ty"]
    half = n_ty // 2

    def lin(a, b, m):
        return (a * n_ty + b) * 2 + m

    def perm(move):
        return [
            (lin(a, b, m), lin(*move(a, b, m)))
            for a in range(n_tx)
            for b in range(n_ty)
            for m in range(2)
        ]

    def side(b, d, m):
        other = (b + d) % n_ty
        return other, (1 - m if b // half != other // half else m)

    return {
        "up": perm(lambda a, b, m: ((a - 1) % n_tx, b, m)),
        "down": perm(lambda a, b, m: ((a + 1) % n_tx, b, m)),
        "left": perm(lambda a, b, m: (a, *side(b, -1, m))),
        "right": perm(lambda a, b, m: (a, *side(b, 1, m))),
        "swap": perm(lambda a, b, m: (a, b, 1 - m)),
    }


def split(x):
    high = x.astype(bf16)
    return high, (x - high.astype(f32)).astype(bf16)


def tables():
    ramp = np.arange(W)
    angle = (ramp[:, None] * ramp[None, :] % W) * (2.0 * math.pi / W)
    cos = np.cos(angle) / math.sqrt(W)
    sin = -np.sin(angle) / math.sqrt(W)
    ahead = np.block([[cos, sin], [-sin, cos]])
    out = []
    for mat in (ahead, ahead.T):
        high = mat.astype(jnp.bfloat16)
        low = (mat - high.astype(np.float64)).astype(jnp.bfloat16)
        out += [high, low]
    return out


def dot(a, b):
    return jnp.dot(a, b, preferred_element_type=f32)


def iota(axis):
    return lax.broadcasted_iota(jnp.int32, (W, W), axis)


def send_body(above, obj, right, left, up_out, down_out):
    m = lax.axis_index("mode")
    last = lax.axis_index("ty") == lax.axis_size("ty") - 1
    first = lax.axis_index("ty") == 0
    col0 = above[2 * m + 1]
    q, s = col0 // W, lax.rem(col0, W)
    lane = iota(1)
    for c in range(2):
        rim = jnp.where(last, 0.0, right[c])
        here = obj[c, :, pl.ds(pl.multiple_of(q * W, W), W)]
        nxt = obj[c, :, pl.ds(pl.multiple_of(jnp.minimum(q + 1, 3) * W, W), W)]
        nxt = jnp.where(q == 3, rim, nxt)
        up_out[c, 0:W, :] = jnp.where(lane >= s, here, nxt)
        for row, out, at in ((0, up_out, W), (W - 1, down_out, 0)):
            for k in range(4):
                out[c, at + k : at + k + 1, :] = obj[c, row : row + 1, k * W : (k + 1) * W]
            out[c, at + 4 : at + 5, :] = jnp.where(last, 0.0, right[c, row : row + 1, :])
            edge = jnp.where(first, 0.0, left[c, row : row + 1, :])
            out[c, at + 5 : at + 6, :] = jnp.concatenate([edge, edge], axis=1)
            out[c, at + 6 : at + 8, :] = jnp.zeros((2, W), f32)


def main_body(
    offs, counts, obj, right, below, probe_a, probe_b, meas, fh, fl, gh, gl, grad_out, spill_out, wave
):
    m = lax.axis_index("mode")
    last_ty = lax.axis_index("ty") == lax.axis_size("ty") - 1
    last_tx = lax.axis_index("tx") == lax.axis_size("tx") - 1
    row0, col0 = offs[2 * m], offs[2 * m + 1]
    q, s = col0 // W, lax.rem(col0, W)
    live = jnp.where(m < counts[0], 1.0, 0.0).astype(f32)
    lane, row = iota(1), iota(0)
    patch = []
    for c in range(2):
        rim = jnp.where(last_ty, 0.0, right[c])
        here = obj[c, :, pl.ds(pl.multiple_of(q * W, W), W)]
        nxt = obj[c, :, pl.ds(pl.multiple_of(jnp.minimum(q + 1, 3) * W, W), W)]
        nxt = jnp.where(q == 3, rim, nxt)
        own = jnp.where(lane >= s, here, nxt)
        low = jnp.where(last_tx, 0.0, below[c, 0:W, :])
        rolled = jnp.where(row >= row0, own, low)
        rolled = pltpu.roll(rolled, lax.rem(W - row0, W), 0)
        patch.append(pltpu.roll(rolled, lax.rem(W - s, W), 1))

    def probe(k, c):
        return (probe_a, probe_b)[k // 2][k % 2, c]

    def rows_times(re, im, high, low):
        rh, rl = split(re)
        ih, il = split(im)
        xh = jnp.concatenate([rh, ih], axis=1)
        xl = jnp.concatenate([rl, il], axis=1)
        return dot(xh, high[...]) + dot(xh, low[...]) + dot(xl, high[...])

    def cols_times(z, high, low):
        y = jnp.concatenate([z[:, :W], z[:, W:]], axis=0)
        yh, yl = split(y)
        return dot(high[...], yh) + dot(low[...], yh) + dot(high[...], yl)

    power = jnp.zeros((W, W), f32)
    for k in range(4):
        pr, pi = probe(k, 0), probe(k, 1)
        z = rows_times(pr * patch[0] - pi * patch[1], pr * patch[1] + pi * patch[0], fh, fl)
        w = cols_times(z, gh, gl)
        wave[k] = w
        power = power + w[:W] * w[:W] + w[W:] * w[W:]
    resid = power - meas[0, 0, m]
    grad = [jnp.zeros((W, W), f32), jnp.zeros((W, W), f32)]
    for k in range(4):
        pr, pi = probe(k, 0), probe(k, 1)
        z = rows_times(resid * wave[k, :W], resid * wave[k, W:], gh, gl)
        b = cols_times(z, fh, fl)
        br, bi = b[:W], b[W:]
        grad[0] = grad[0] + pr * br + pi * bi
        grad[1] = grad[1] + pr * bi - pi * br
    spills = (q == 3) & (lane < s)
    mark = jnp.where(row >= row0, 1.0, 0.0).astype(f32)
    for c in range(2):
        g = pltpu.roll(pltpu.roll(grad[c] * live, row0, 0), s, 1)
        grad_out[c] = g
        spill_out[c] = jnp.where(lane == W - 1, mark, jnp.where(spills, g, 0.0))


def prior_body(gram, obj, right, left, up, down, out):
    tx, ty = lax.axis_index("tx"), lax.axis_index("ty")
    n_tx, n_ty = lax.axis_size("tx"), lax.axis_size("ty")
    cols = obj.shape[2]
    shape = (W, cols)
    lane = lax.broadcasted_iota(jnp.int32, shape, 1)
    row = lax.broadcasted_iota(jnp.int32, shape, 0)
    g = [[gram[4 * i + j] for j in range(4)] for i in range(4)]

    def beside(x, before, after):
        one_left = jnp.where(lane == 0, before, pltpu.roll(x, 1, 1))
        one_right = jnp.where(lane == cols - 1, after, pltpu.roll(x, cols - 1, 1))
        return one_left, one_right

    for c in range(2):
        x = obj[c]
        after = jnp.where(ty == n_ty - 1, 0.0, right[c, :, 0:1])
        before = jnp.where(ty == 0, 0.0, left[c, :, 127:128])

        def line(ref, flag):
            whole = jnp.concatenate([ref[c, k : k + 1, :] for k in range(4)], axis=1)
            return (
                jnp.where(flag, 0.0, whole),
                jnp.where(flag, 0.0, ref[c, 5:6, W - 1 : W]),
                jnp.where(flag, 0.0, ref[c, 4:5, 0:1]),
            )

        u_mid, u_left, u_right = line(up, tx == 0)
        d_mid, d_left, d_right = line(down, tx == n_tx - 1)
        row1 = lax.broadcasted_iota(jnp.int32, (W, 1), 0)
        xl, xr = beside(x, before, after)

        def above(mid, edge):
            return jnp.where(row == 0, edge, pltpu.roll(mid, 1, 0))

        def under(mid, edge):
            return jnp.where(row == W - 1, edge, pltpu.roll(mid, W - 1, 0))

        def shift_line(mid, b, a):
            l1 = lax.broadcasted_iota(jnp.int32, (1, cols), 1)
            return (
                jnp.where(l1 == 0, b, pltpu.roll(mid, 1, 1)),
                jnp.where(l1 == cols - 1, a, pltpu.roll(mid, cols - 1, 1)),
            )

        ul, ur = shift_line(u_mid, u_left, u_right)
        dl, dr = shift_line(d_mid, d_left, d_right)
        xu, xd = above(x, u_mid), under(x, d_mid)
        xul, xur = above(xl, ul), above(xr, ur)
        xdl, xdr = under(xl, dl), under(xr, dr)
        in_col = (lane > 0) | (ty > 0)
        in_row = (row > 0) | (tx > 0)
        total = g[0][0] * x + g[0][1] * xr + g[0][2] * xd + g[0][3] * xdr
        total += jnp.where(in_col, g[1][0] * xl + g[1][1] * x + g[1][2] * xdl + g[1][3] * xd, 0.0)
        total += jnp.where(in_row, g[2][0] * xu + g[2][1] * xur + g[2][2] * x + g[2][3] * xr, 0.0)
        total += jnp.where(
            in_row & in_col, g[3][0] * xul + g[3][1] * xu + g[3][2] * xl + g[3][3] * x, 0.0
        )
        out[c] = x - step_size * total


def lower_body(one, two, out):
    first = lax.axis_index("ty") == 0
    lane = iota(1)
    for c in range(2):
        total = jnp.zeros((W, W), f32)
        for ref in (one, two):
            keep = (ref[c, :, W - 1 : W] < 0.5) & (lane < W - 1)
            total = total + jnp.where(keep, ref[c], 0.0)
        out[c] = jnp.where(first, 0.0, total)


def final_body(offs, above, base, own_m, own_p, left_m, left_p, up_m, up_p, corner, out):
    m = lax.axis_index("mode")
    tx, ty = lax.axis_index("tx"), lax.axis_index("ty")
    lane, row = iota(1), iota(0)
    out[...] = base[...]
    for c in range(2):
        for ref in (left_m, left_p):
            keep = (ref[c, :, W - 1 : W] > 0.5) & (lane < W - 1) & (ty > 0)
            out[c, :, 0:W] = out[c, :, 0:W] - step_size * jnp.where(keep, ref[c], 0.0)
        out[c, :, 0:W] = out[c, :, 0:W] - step_size * jnp.where(tx > 0, corner[c], 0.0)
        for ref, table, slot, mine in (
            (own_m, offs, m, True),
            (own_p, offs, 1 - m, True),
            (up_m, above, m, False),
            (up_p, above, 1 - m, False),
        ):
            row0, col0 = table[2 * slot], table[2 * slot + 1]
            q, s = col0 // W, lax.rem(col0, W)
            rows = (row >= row0) if mine else ((row < row0) & (tx > 0))
            here = pl.ds(pl.multiple_of(q * W, W), W)
            out[c, :, here] = out[c, :, here] - step_size * jnp.where(rows & (lane >= s), ref[c], 0.0)
            nxt = pl.ds(pl.multiple_of(jnp.minimum(q + 1, 3) * W, W), W)
            keep = rows & (lane < s) & (q < 3)
            out[c, :, nxt] = out[c, :, nxt] - step_size * jnp.where(keep, ref[c], 0.0)


def call(body, name, shapes, in_specs, flops, bytes_accessed, scratch=()):
    many = isinstance(shapes, list)
    outs = [jax.ShapeDtypeStruct(s, f32) for s in (shapes if many else [shapes])]
    return pl.pallas_call(
        body,
        name=name,
        out_shape=outs if many else outs[0],
        in_specs=in_specs,
        out_specs=[VMEM] * len(outs) if many else VMEM,
        scratch_shapes=list(scratch),
        compiler_params=pltpu.CompilerParams(vmem_limit_bytes=56 << 20),
        cost_estimate=pl.CostEstimate(flops=flops, bytes_accessed=bytes_accessed, transcendentals=0),
    )


def local(ring, obj, probe, intensity, offsets, counts, filters):
    def go(value, where):
        return lax.ppermute(value, axes, ring[where])

    rows, cols = obj.shape[1:]
    piece = (2, W, W)
    offs = offsets.reshape(4)
    live = counts.reshape(1)
    right = go(obj[:, :, :W], "left")
    above = go(offs, "down")
    probe_b = go(probe, "swap")
    left = go(obj[:, :, cols - 128 :], "right")
    gram = jnp.dot(filters.T, filters, precision=lax.Precision.HIGHEST).reshape(16)
    to_up, to_down = call(
        send_body, "send", [(2, W + 8, W), (2, 8, W)], [SMEM] + [VMEM] * 3, 1 << 20, 4 << 20
    )(above, obj, right, left)
    below = go(to_up, "up")
    over = go(to_down, "down")
    grad, spill = call(
        main_body,
        "main",
        [piece, piece],
        [SMEM, SMEM] + [VMEM] * 10,
        10 << 30,
        12 << 20,
        [pltpu.VMEM((4, 2 * W, W), f32)],
    )(offs, live, obj, right, below, probe, probe_b, intensity, *[jnp.asarray(t) for t in tables()])
    grad_p = go(grad, "swap")
    left_m = go(spill, "right")
    up_m = go(grad, "down")
    base = call(prior_body, "prior", (2, rows, cols), [SMEM] + [VMEM] * 5, 1 << 25, 5 << 20)(
        gram, obj, right, left, over, below[:, W:, :]
    )
    left_p = go(left_m, "swap")
    up_p = go(grad_p, "down")
    lower = call(lower_body, "lower", piece, [VMEM] * 2, 1 << 20, 3 << 19)(left_m, left_p)
    corner = go(lower, "down")
    return call(final_body, "final", (2, rows, cols), [SMEM, SMEM] + [VMEM] * 8, 1 << 24, 8 << 20)(
        offs, above, base, grad, grad_p, left_m, left_p, up_m, up_p, corner
    )


def solution(mesh):
    placed = (
        P(None, "tx", "ty"),
        P("mode", None, None, None),
        P("tx", "ty", None, None, None),
        P("tx", "ty", None, None),
        P("tx", "ty"),
        P(),
    )
    return jax.shard_map(
        functools.partial(local, rings(mesh)),
        mesh=mesh,
        in_specs=placed,
        out_specs=P(None, "tx", "ty"),
        check_vma=False,
    )
```

```python
import functools
import math

import jax
import jax.numpy as jnp
import numpy as np
from jax import lax
from jax.experimental import pallas as pl
from jax.experimental.pallas import tpu as pltpu
from jax.sharding import PartitionSpec as P


W = 256
axes = ("tx", "ty", "mode")
step_size = 0.25
f32 = jnp.float32
bf16 = jnp.bfloat16
VMEM = pl.BlockSpec(memory_space=pltpu.VMEM)
SMEM = pl.BlockSpec(memory_space=pltpu.SMEM)


def rings(mesh):
    n_tx, n_ty = mesh.shape["tx"], mesh.shape["ty"]
    half = n_ty // 2

    def lin(a, b, m):
        return (a * n_ty + b) * 2 + m

    def perm(move):
        return [
            (lin(a, b, m), lin(*move(a, b, m)))
            for a in range(n_tx)
            for b in range(n_ty)
            for m in range(2)
        ]

    def side(b, d, m):
        other = (b + d) % n_ty
        return other, (1 - m if b // half != other // half else m)

    return {
        "up": perm(lambda a, b, m: ((a - 1) % n_tx, b, m)),
        "down": perm(lambda a, b, m: ((a + 1) % n_tx, b, m)),
        "left": perm(lambda a, b, m: (a, *side(b, -1, m))),
        "right": perm(lambda a, b, m: (a, *side(b, 1, m))),
        "core": perm(lambda a, b, m: (a ^ 1, b, m)),
        "swap": perm(lambda a, b, m: (a, b, 1 - m)),
    }


def split(x):
    high = x.astype(bf16)
    return high, (x - high.astype(f32)).astype(bf16)


def tables():
    half = W // 2
    k, l = np.arange(half)[:, None], np.arange(half)[None, :]
    out = []
    for shift in (0, 1):
        angle = (k * (2 * l + shift) % W) * (2.0 * math.pi / W)
        re, im = np.cos(angle) / math.sqrt(W), -np.sin(angle) / math.sqrt(W)
        block = np.block([[re, im], [-im, re]])
        for mat in (block, block.T):
            high = mat.astype(jnp.bfloat16)
            out += [high, (mat - high.astype(np.float64)).astype(jnp.bfloat16)]
    return out


def dot(a, b):
    return jnp.dot(a, b, preferred_element_type=f32)


def rows_times(x, table):
    xh, xl = split(x)
    high, low = table
    return dot(xh, high) + dot(xh, low) + dot(xl, high)


def cols_times(table, x):
    xh, xl = split(x)
    high, low = table
    return dot(high, xh) + dot(low, xh) + dot(high, xl)


def forward(re, im, even, even_t, odd, odd_t):
    h = W // 2

    def lanes(x, y):
        return jnp.concatenate([x, y], axis=1)

    def stack(x, y):
        return jnp.concatenate([x, y], axis=0)

    e = rows_times(lanes(re[:, :h] + re[:, h:], im[:, :h] + im[:, h:]), even)
    o = rows_times(lanes(re[:, :h] - re[:, h:], im[:, :h] - im[:, h:]), odd)
    re, im = lanes(e[:, :h], o[:, :h]), lanes(e[:, h:], o[:, h:])
    e = cols_times(even_t, stack(re[:h] + re[h:], im[:h] + im[h:]))
    o = cols_times(odd_t, stack(re[:h] - re[h:], im[:h] - im[h:]))
    return stack(e[:h], o[:h]), stack(e[h:], o[h:])


def backward(re, im, even, even_t, odd, odd_t):
    h = W // 2

    def lanes(x, y):
        return jnp.concatenate([x, y], axis=1)

    def stack(x, y):
        return jnp.concatenate([x, y], axis=0)

    a = rows_times(lanes(re[:, :h], im[:, :h]), even_t)
    b = rows_times(lanes(re[:, h:], im[:, h:]), odd_t)
    p, n = a + b, a - b
    re, im = lanes(p[:, :h], n[:, :h]), lanes(p[:, h:], n[:, h:])
    a = cols_times(even, stack(re[:h], im[:h]))
    b = cols_times(odd, stack(re[h:], im[h:]))
    p, n = a + b, a - b
    return stack(p[:h], n[:h]), stack(p[h:], n[h:])


def iota(axis):
    return lax.broadcasted_iota(jnp.int32, (W, W), axis)


def window(obj, c, right, q, s):
    lane = iota(1)
    last = lax.axis_index("ty") == lax.axis_size("ty") - 1
    here = obj[c, :, pl.ds(pl.multiple_of(q * W, W), W)]
    nxt = obj[c, :, pl.ds(pl.multiple_of(jnp.minimum(q + 1, 3) * W, W), W)]
    nxt = jnp.where(q == 3, jnp.where(last, 0.0, right[...]), nxt)
    return jnp.where(lane >= s, here, nxt)


def place(table, slot):
    col0 = table[2 * slot + 1]
    return table[2 * slot], col0 // W, lax.rem(col0, W)


def rim_rows(obj, c, row, right, left):
    last = lax.axis_index("ty") == lax.axis_size("ty") - 1
    first = lax.axis_index("ty") == 0
    edge = jnp.where(first, 0.0, left[c, row : row + 1, :])
    parts = [obj[c, row : row + 1, k * W : (k + 1) * W] for k in range(4)]
    parts.append(jnp.where(last, 0.0, right[row : row + 1, :]))
    parts.append(jnp.concatenate([edge, edge], axis=1))
    return parts


def send_body(c, above, obj, left, *refs):
    rights, up_out = refs[: c + 1], refs[c + 1]
    _, q, s = place(above, lax.axis_index("mode"))
    up_out[0:W, :] = window(obj, c, rights[c], q, s)
    for k, part in enumerate(rim_rows(obj, c, 0, rights[c], left)):
        up_out[W + k : W + k + 1, :] = part
    up_out[W + 6 : W + 8, :] = jnp.zeros((2, W), f32)
    if c == 1:
        down_out = refs[c + 2]
        for d in range(2):
            for k, part in enumerate(rim_rows(obj, d, W - 1, rights[d], left)):
                down_out[d, k : k + 1, :] = part
            down_out[d, 6:8, :] = jnp.zeros((2, W), f32)


def main_body(offs, counts, obj, right_0, right_1, below_0, below_1, probe_a, probe_b, probe_c, meas, *refs):
    mats, (grad_0, grad_1, spill_0, spill_1, wave) = refs[:8], refs[8:]
    m = lax.axis_index("mode")
    last_tx = lax.axis_index("tx") == lax.axis_size("tx") - 1
    row0, q, s = place(offs, m)
    live = jnp.where(m < counts[0], 1.0, 0.0).astype(f32)
    lane, row = iota(1), iota(0)
    patch = []
    for c, right, below in ((0, right_0, below_0), (1, right_1, below_1)):
        low = jnp.where(last_tx, 0.0, below[0:W, :])
        rolled = jnp.where(row >= row0, window(obj, c, right, q, s), low)
        rolled = pltpu.roll(rolled, lax.rem(W - row0, W), 0)
        patch.append(pltpu.roll(rolled, lax.rem(W - s, W), 1))

    def probe(k, c):
        return (probe_a[0, c], probe_a[1, c], probe_b[0, c], probe_c[0, c])[k]

    tabs = [(mats[2 * k][...], mats[2 * k + 1][...]) for k in range(4)]
    power = jnp.zeros((W, W), f32)
    for k in range(4):
        pr, pi = probe(k, 0), probe(k, 1)
        wr, wi = forward(pr * patch[0] - pi * patch[1], pr * patch[1] + pi * patch[0], *tabs)
        wave[k, 0] = wr
        wave[k, 1] = wi
        power = power + wr * wr + wi * wi
    resid = power - meas[...]
    grad = [jnp.zeros((W, W), f32), jnp.zeros((W, W), f32)]
    for k in range(4):
        pr, pi = probe(k, 0), probe(k, 1)
        br, bi = backward(resid * wave[k, 0], resid * wave[k, 1], *tabs)
        grad[0] = grad[0] + pr * br + pi * bi
        grad[1] = grad[1] + pr * bi - pi * br
    mark = jnp.where(row >= row0, 1.0, 0.0).astype(f32)
    for g, grad_out, spill_out in ((grad[0], grad_0, spill_0), (grad[1], grad_1, spill_1)):
        g = pltpu.roll(pltpu.roll(g * live, row0, 0), s, 1)
        grad_out[...] = g
        spill_out[...] = jnp.where(lane == W - 1, mark, jnp.where((q == 3) & (lane < s), g, 0.0))


def sort_body(meas, out):
    m = lax.axis_index("mode")
    h = W // 2
    lane, row = iota(1), iota(0)

    def nth(k):
        return jnp.where(k < h, 2 * k, 2 * k - W + 1)

    pick_cols = jnp.where(row == nth(lane), 1.0, 0.0).astype(bf16)
    pick_rows = jnp.where(lane == nth(row), 1.0, 0.0).astype(bf16)

    def parts(x):
        for _ in range(3):
            part = x.astype(bf16)
            x = x - part.astype(f32)
            yield part

    x = sum(dot(part, pick_cols) for part in parts(meas[0, 0, m]))
    out[...] = sum(dot(pick_rows, part) for part in parts(x))


def spill_body(offs, grad, out):
    row0, q, s = place(offs, 1 - lax.axis_index("mode"))
    lane = iota(1)
    mark = jnp.where(iota(0) >= row0, 1.0, 0.0).astype(f32)
    out[...] = jnp.where(lane == W - 1, mark, jnp.where((q == 3) & (lane < s), grad[...], 0.0))


def take(out, c, ref, spot, rows):
    _, q, s = spot
    lane = iota(1)
    value = ref[...]
    here = pl.ds(pl.multiple_of(q * W, W), W)
    out[c, :, here] = out[c, :, here] - step_size * jnp.where(rows & (lane >= s), value, 0.0)
    nxt = pl.ds(pl.multiple_of(jnp.minimum(q + 1, 3) * W, W), W)
    keep = rows & (lane < s) & (q < 3)
    out[c, :, nxt] = out[c, :, nxt] - step_size * jnp.where(keep, value, 0.0)


def prior_body(gram, offs, obj, right_0, right_1, left, up, below_0, below_1, own_0, own_1, out):
    tx, ty = lax.axis_index("tx"), lax.axis_index("ty")
    n_tx, n_ty = lax.axis_size("tx"), lax.axis_size("ty")
    cols = obj.shape[2]
    shape = (W, cols)
    lane = lax.broadcasted_iota(jnp.int32, shape, 1)
    row = lax.broadcasted_iota(jnp.int32, shape, 0)
    g = [[gram[4 * i + j] for j in range(4)] for i in range(4)]

    def beside(x, before, after):
        one_left = jnp.where(lane == 0, before, pltpu.roll(x, 1, 1))
        one_right = jnp.where(lane == cols - 1, after, pltpu.roll(x, cols - 1, 1))
        return one_left, one_right

    spot = place(offs, lax.axis_index("mode"))
    for c, right, below, own in ((0, right_0, below_0, own_0), (1, right_1, below_1, own_1)):
        x = obj[c]
        after = jnp.where(ty == n_ty - 1, 0.0, right[:, 0:1])
        before = jnp.where(ty == 0, 0.0, left[c, :, 127:128])

        def line(rim, flag):
            rim = jnp.where(flag, 0.0, rim)
            whole = jnp.concatenate([rim[k : k + 1, :] for k in range(4)], axis=1)
            return whole, rim[5:6, W - 1 : W], rim[4:5, 0:1]

        u_mid, u_left, u_right = line(up[c], tx == 0)
        d_mid, d_left, d_right = line(below[W : W + 8, :], tx == n_tx - 1)
        xl, xr = beside(x, before, after)

        def above(mid, edge):
            return jnp.where(row == 0, edge, pltpu.roll(mid, 1, 0))

        def under(mid, edge):
            return jnp.where(row == W - 1, edge, pltpu.roll(mid, W - 1, 0))

        def shift_line(mid, b, a):
            l1 = lax.broadcasted_iota(jnp.int32, (1, cols), 1)
            return (
                jnp.where(l1 == 0, b, pltpu.roll(mid, 1, 1)),
                jnp.where(l1 == cols - 1, a, pltpu.roll(mid, cols - 1, 1)),
            )

        ul, ur = shift_line(u_mid, u_left, u_right)
        dl, dr = shift_line(d_mid, d_left, d_right)
        xu, xd = above(x, u_mid), under(x, d_mid)
        xul, xur = above(xl, ul), above(xr, ur)
        xdl, xdr = under(xl, dl), under(xr, dr)
        in_col = (lane > 0) | (ty > 0)
        in_row = (row > 0) | (tx > 0)
        total = g[0][0] * x + g[0][1] * xr + g[0][2] * xd + g[0][3] * xdr
        total += jnp.where(in_col, g[1][0] * xl + g[1][1] * x + g[1][2] * xdl + g[1][3] * xd, 0.0)
        total += jnp.where(in_row, g[2][0] * xu + g[2][1] * xur + g[2][2] * x + g[2][3] * xr, 0.0)
        total += jnp.where(
            in_row & in_col, g[3][0] * xul + g[3][1] * xu + g[3][2] * xl + g[3][3] * x, 0.0
        )
        out[c] = x - step_size * total
        take(out, c, own, spot, iota(0) >= spot[0])


def lower_body(one, two, out):
    first = lax.axis_index("ty") == 0
    lane = iota(1)
    total = jnp.zeros((W, W), f32)
    for ref in (one, two):
        keep = (ref[:, W - 1 : W] < 0.5) & (lane < W - 1)
        total = total + jnp.where(keep, ref[...], 0.0)
    out[...] = jnp.where(first, 0.0, total)


def mid_body(offs, above, base, *refs):
    own_p, left_m, left_p, up_m, up_p = (refs[2 * k : 2 * k + 2] for k in range(5))
    out = refs[10]
    m = lax.axis_index("mode")
    tx, ty = lax.axis_index("tx"), lax.axis_index("ty")
    lane, row = iota(1), iota(0)
    out[...] = base[...]
    mine, from_m, from_p = place(offs, 1 - m), place(above, m), place(above, 1 - m)
    for c in range(2):
        for pair in (left_m, left_p):
            ref = pair[c]
            keep = (ref[:, W - 1 : W] > 0.5) & (lane < W - 1) & (ty > 0)
            out[c, :, 0:W] = out[c, :, 0:W] - step_size * jnp.where(keep, ref[...], 0.0)
        take(out, c, own_p[c], mine, row >= mine[0])
        take(out, c, up_m[c], from_m, (row < from_m[0]) & (tx > 0))
        take(out, c, up_p[c], from_p, (row < from_p[0]) & (tx > 0))


def final_body(mid, corner_0, corner_1, out, buf, sems):
    tx = lax.axis_index("tx")
    loads = [pltpu.make_async_copy(mid.at[c, :, 0:W], buf.at[c], sems.at[c]) for c in range(2)]
    stores = [pltpu.make_async_copy(buf.at[c], out.at[c, :, 0:W], sems.at[2 + c]) for c in range(2)]
    for load in loads:
        load.start()
    for c, corner in enumerate((corner_0, corner_1)):
        loads[c].wait()
        buf[c] = buf[c] - step_size * jnp.where(tx > 0, corner[...], 0.0)
        stores[c].start()
    for store in stores:
        store.wait()


def call(body, shapes, in_specs, limit, flops, bytes_accessed, scratch=(), out_spec=VMEM, aliases={}):
    many = isinstance(shapes, list)
    outs = [jax.ShapeDtypeStruct(s, f32) for s in (shapes if many else [shapes])]
    return pl.pallas_call(
        body,
        out_shape=outs if many else outs[0],
        in_specs=in_specs,
        out_specs=[out_spec] * len(outs) if many else out_spec,
        scratch_shapes=list(scratch),
        input_output_aliases=aliases,
        compiler_params=pltpu.CompilerParams(vmem_limit_bytes=limit << 20),
        cost_estimate=pl.CostEstimate(flops=flops, bytes_accessed=bytes_accessed, transcendentals=0),
    )


def local(ring, obj, probe, intensity, offsets, counts, filters):
    def go(value, where):
        return lax.ppermute(value, axes, ring[where])

    tabs = [jnp.asarray(t) for t in tables()]

    rows, cols = obj.shape[1:]
    piece = (W, W)
    whole = (2, rows, cols)
    offs = offsets.reshape(4)
    live = counts.reshape(1)
    above = go(offs, "down")
    right = [go(obj[c, :, :W], "left") for c in range(2)]
    left = go(obj[:, :, cols - 128 :], "right")
    core = lax.rem(lax.axis_index("tx"), 2)
    probe_b = go(lax.dynamic_slice_in_dim(probe, core, 1, 0), "swap")
    probe_c = go(probe_b, "core")
    gram = jnp.dot(filters.T, filters, precision=lax.Precision.HIGHEST).reshape(16)
    meas = call(sort_body, piece, [VMEM], 8, 1 << 26, 3 << 18)(intensity)
    up_0 = call(
        functools.partial(send_body, 0), (W + 8, W), [SMEM] + [VMEM] * 3, 16, 1 << 20, 2 << 20
    )(above, obj, left, right[0])
    below_0 = go(up_0, "up")
    up_1, rim = call(
        functools.partial(send_body, 1),
        [(W + 8, W), (2, 8, W)],
        [SMEM] + [VMEM] * 4,
        16,
        1 << 20,
        2 << 20,
    )(above, obj, left, *right)
    below_1 = go(up_1, "up")
    over = go(rim, "down")
    below_0, below_1, over = lax.optimization_barrier((below_0, below_1, over))
    g0, g1, s0, s1 = call(
        main_body,
        [piece] * 4,
        [SMEM, SMEM] + [VMEM] * 17,
        16,
        5 << 30,
        12 << 20,
        [pltpu.VMEM((4, 2, W, W), f32)],
    )(offs, live, obj, *right, below_0, below_1, probe, probe_b, probe_c, meas, *tabs)
    p1 = go(g1, "swap")
    m0 = go(s0, "right")
    p0 = go(g0, "swap")
    m1 = go(s1, "right")
    b0, b1 = go(g0, "down"), go(g1, "down")
    base = call(prior_body, whole, [SMEM, SMEM] + [VMEM] * 9, 16, 1 << 28, 16 << 20)(
        gram, offs, obj, *right, left, over, below_0, below_1, g0, g1
    )
    n1 = go(call(spill_body, piece, [SMEM, VMEM], 8, 1 << 18, 1 << 19)(offs, p1), "right")
    n0 = go(m0, "swap")
    c1, c0 = go(p1, "down"), go(p0, "down")
    corner = [
        go(call(lower_body, piece, [VMEM] * 2, 8, 1 << 18, 3 << 18)(a, b), "down")
        for a, b in ((m0, n0), (m1, n1))
    ]
    mid = call(mid_body, whole, [SMEM, SMEM] + [VMEM] * 11, 12, 1 << 24, 10 << 20)(
        offs, above, base, p0, p1, m0, m1, n0, n1, b0, b1, c0, c1
    )
    any_space = pl.BlockSpec(memory_space=pl.ANY)
    return call(
        final_body,
        whole,
        [any_space, VMEM, VMEM],
        8,
        1 << 18,
        2 << 20,
        [pltpu.VMEM((2, W, W), f32), pltpu.SemaphoreType.DMA((4,))],
        any_space,
        {0: 0},
    )(mid, *corner)


def solution(mesh):
    placed = (
        P(None, "tx", "ty"),
        P("mode", None, None, None),
        P("tx", "ty", None, None, None),
        P("tx", "ty", None, None),
        P("tx", "ty"),
        P(),
    )

    def body(*args):
        return local(rings(mesh), *args)

    return jax.shard_map(
        body, mesh=mesh, in_specs=placed, out_specs=P(None, "tx", "ty"), check_vma=False
    )
```

```python
import functools
import math

import jax
import jax.numpy as jnp
import numpy as np
from jax import lax
from jax.experimental import pallas as pl
from jax.experimental.pallas import tpu as pltpu
from jax.sharding import PartitionSpec as P


W = 256
axes = ("tx", "ty", "mode")
step_size = 0.25
f32 = jnp.float32
bf16 = jnp.bfloat16
VMEM = pl.BlockSpec(memory_space=pltpu.VMEM)
SMEM = pl.BlockSpec(memory_space=pltpu.SMEM)


def rings(mesh):
    n_tx, n_ty = mesh.shape["tx"], mesh.shape["ty"]
    half = n_ty // 2

    def lin(a, b, m):
        return (a * n_ty + b) * 2 + m

    def perm(move):
        return [
            (lin(a, b, m), lin(*move(a, b, m)))
            for a in range(n_tx)
            for b in range(n_ty)
            for m in range(2)
        ]

    def side(b, d, m):
        other = (b + d) % n_ty
        return other, (1 - m if b // half != other // half else m)

    return {
        "up": perm(lambda a, b, m: ((a - 1) % n_tx, b, m)),
        "down": perm(lambda a, b, m: ((a + 1) % n_tx, b, m)),
        "left": perm(lambda a, b, m: (a, *side(b, -1, m))),
        "right": perm(lambda a, b, m: (a, *side(b, 1, m))),
        "core": perm(lambda a, b, m: (a ^ 1, b, m)),
        "swap": perm(lambda a, b, m: (a, b, 1 - m)),
    }


def split(x):
    high = x.astype(bf16)
    return high, (x - high.astype(f32)).astype(bf16)


def tables():
    half = W // 2
    k, l = np.arange(half)[:, None], np.arange(half)[None, :]
    out = []
    for shift in (0, 1):
        angle = (k * (2 * l + shift) % W) * (2.0 * math.pi / W)
        re, im = np.cos(angle) / math.sqrt(W), -np.sin(angle) / math.sqrt(W)
        block = np.block([[re, im], [-im, re]])
        for mat in (block, block.T):
            high = mat.astype(jnp.bfloat16)
            out += [high, (mat - high.astype(np.float64)).astype(jnp.bfloat16)]
    return out


def dot(a, b):
    return jnp.dot(a, b, preferred_element_type=f32)


def rows_times(x, table):
    xh, xl = split(x)
    high, low = table
    return dot(xh, high) + dot(xh, low) + dot(xl, high)


def cols_times(table, x):
    xh, xl = split(x)
    high, low = table
    return dot(high, xh) + dot(low, xh) + dot(high, xl)


def forward(re, im, even, even_t, odd, odd_t):
    h = W // 2

    def lanes(x, y):
        return jnp.concatenate([x, y], axis=1)

    def stack(x, y):
        return jnp.concatenate([x, y], axis=0)

    e = rows_times(lanes(re[:, :h] + re[:, h:], im[:, :h] + im[:, h:]), even)
    o = rows_times(lanes(re[:, :h] - re[:, h:], im[:, :h] - im[:, h:]), odd)
    re, im = lanes(e[:, :h], o[:, :h]), lanes(e[:, h:], o[:, h:])
    e = cols_times(even_t, stack(re[:h] + re[h:], im[:h] + im[h:]))
    o = cols_times(odd_t, stack(re[:h] - re[h:], im[:h] - im[h:]))
    return stack(e[:h], o[:h]), stack(e[h:], o[h:])


def backward(re, im, even, even_t, odd, odd_t):
    h = W // 2

    def lanes(x, y):
        return jnp.concatenate([x, y], axis=1)

    def stack(x, y):
        return jnp.concatenate([x, y], axis=0)

    a = rows_times(lanes(re[:, :h], im[:, :h]), even_t)
    b = rows_times(lanes(re[:, h:], im[:, h:]), odd_t)
    p, n = a + b, a - b
    re, im = lanes(p[:, :h], n[:, :h]), lanes(p[:, h:], n[:, h:])
    a = cols_times(even, stack(re[:h], im[:h]))
    b = cols_times(odd, stack(re[h:], im[h:]))
    p, n = a + b, a - b
    return stack(p[:h], n[:h]), stack(p[h:], n[h:])


def iota(axis):
    return lax.broadcasted_iota(jnp.int32, (W, W), axis)


def window(obj, c, right, q, s):
    lane = iota(1)
    last = lax.axis_index("ty") == lax.axis_size("ty") - 1
    here = obj[c, :, pl.ds(pl.multiple_of(q * W, W), W)]
    nxt = obj[c, :, pl.ds(pl.multiple_of(jnp.minimum(q + 1, 3) * W, W), W)]
    nxt = jnp.where(q == 3, jnp.where(last, 0.0, right[...]), nxt)
    return jnp.where(lane >= s, here, nxt)


def place(table, slot):
    col0 = table[slot, 1]
    return table[slot, 0], col0 // W, lax.rem(col0, W)


def rim_rows(obj, c, row, right, left):
    last = lax.axis_index("ty") == lax.axis_size("ty") - 1
    first = lax.axis_index("ty") == 0
    edge = jnp.where(first, 0.0, left[c, row : row + 1, :])
    parts = [obj[c, row : row + 1, k * W : (k + 1) * W] for k in range(4)]
    parts.append(jnp.where(last, 0.0, right[row : row + 1, :]))
    parts.append(jnp.concatenate([edge, edge], axis=1))
    return parts


def send_body(c, above, obj, right, out):
    _, q, s = place(above, lax.axis_index("mode"))
    out[...] = window(obj, c, right, q, s)


def rim_body(obj, left, right_0, right_1, up_out, down_out):
    for c, right in enumerate((right_0, right_1)):
        for row, out in ((0, up_out), (W - 1, down_out)):
            for k, part in enumerate(rim_rows(obj, c, row, right, left)):
                out[c, k : k + 1, :] = part
            out[c, 6:8, :] = jnp.zeros((2, W), f32)


def main_body(offs, counts, obj, right_0, right_1, below_0, below_1, probe_a, probe_b, probe_c, meas, *refs):
    mats, (grad_0, grad_1, spill_0, spill_1, keep_0, keep_1, wave) = refs[:8], refs[8:]
    m = lax.axis_index("mode")
    last_tx = lax.axis_index("tx") == lax.axis_size("tx") - 1
    row0, q, s = place(offs, m)
    live = jnp.where(m < counts[0, 0], 1.0, 0.0).astype(f32)
    lane, row = iota(1), iota(0)
    patch = []
    for c, right, below in ((0, right_0, below_0), (1, right_1, below_1)):
        low = jnp.where(last_tx, 0.0, below[...])
        rolled = jnp.where(row >= row0, window(obj, c, right, q, s), low)
        rolled = pltpu.roll(rolled, lax.rem(W - row0, W), 0)
        patch.append(pltpu.roll(rolled, lax.rem(W - s, W), 1))

    def probe(k, c):
        return (probe_a[0, c], probe_a[1, c], probe_b[0, c], probe_c[0, c])[k]

    tabs = [(mats[2 * k][...], mats[2 * k + 1][...]) for k in range(4)]
    power = jnp.zeros((W, W), f32)
    for k in range(4):
        pr, pi = probe(k, 0), probe(k, 1)
        wr, wi = forward(pr * patch[0] - pi * patch[1], pr * patch[1] + pi * patch[0], *tabs)
        wave[k, 0] = wr
        wave[k, 1] = wi
        power = power + wr * wr + wi * wi
    resid = power - meas[...]
    grad = [jnp.zeros((W, W), f32), jnp.zeros((W, W), f32)]
    for k in range(4):
        pr, pi = probe(k, 0), probe(k, 1)
        br, bi = backward(resid * wave[k, 0], resid * wave[k, 1], *tabs)
        grad[0] = grad[0] + pr * br + pi * bi
        grad[1] = grad[1] + pr * bi - pi * br
    mark = jnp.where(row >= row0, 1.0, 0.0).astype(f32)
    for g, grad_out, spill_out, keep_out in (
        (grad[0], grad_0, spill_0, keep_0),
        (grad[1], grad_1, spill_1, keep_1),
    ):
        g = pltpu.roll(pltpu.roll(g * live, row0, 0), s, 1)
        grad_out[...] = g
        keep_out[...] = g
        spill_out[...] = jnp.where(lane == W - 1, mark, jnp.where((q == 3) & (lane < s), g, 0.0))


def sort_body(meas, out):
    m = lax.axis_index("mode")
    h = W // 2
    lane, row = iota(1), iota(0)

    def nth(k):
        return jnp.where(k < h, 2 * k, 2 * k - W + 1)

    pick_cols = jnp.where(row == nth(lane), 1.0, 0.0).astype(bf16)
    pick_rows = jnp.where(lane == nth(row), 1.0, 0.0).astype(bf16)

    def parts(x):
        for _ in range(3):
            part = x.astype(bf16)
            x = x - part.astype(f32)
            yield part

    x = sum(dot(part, pick_cols) for part in parts(meas[0, 0, m]))
    out[...] = sum(dot(pick_rows, part) for part in parts(x))


def spill_body(offs, grad, out):
    row0, q, s = place(offs, 1 - lax.axis_index("mode"))
    lane = iota(1)
    mark = jnp.where(iota(0) >= row0, 1.0, 0.0).astype(f32)
    out[...] = jnp.where(lane == W - 1, mark, jnp.where((q == 3) & (lane < s), grad[...], 0.0))


def take(out, c, ref, spot, rows):
    _, q, s = spot
    lane = iota(1)
    value = ref[...]
    here = pl.ds(pl.multiple_of(q * W, W), W)
    out[c, :, here] = out[c, :, here] - step_size * jnp.where(rows & (lane >= s), value, 0.0)
    nxt = pl.ds(pl.multiple_of(jnp.minimum(q + 1, 3) * W, W), W)
    keep = rows & (lane < s) & (q < 3)
    out[c, :, nxt] = out[c, :, nxt] - step_size * jnp.where(keep, value, 0.0)


def prior_body(filt, offs, obj, right_0, right_1, left, up, down, own_0, own_1, out):
    tx, ty = lax.axis_index("tx"), lax.axis_index("ty")
    n_tx, n_ty = lax.axis_size("tx"), lax.axis_size("ty")
    cols = obj.shape[2]
    shape = (W, cols)
    lane = lax.broadcasted_iota(jnp.int32, shape, 1)
    row = lax.broadcasted_iota(jnp.int32, shape, 0)
    taps = [[filt[i, k] for i in range(4)] for k in range(filt.shape[1])]
    g = [[sum(tap[i] * tap[j] for tap in taps) for j in range(4)] for i in range(4)]

    def beside(x, before, after):
        one_left = jnp.where(lane == 0, before, pltpu.roll(x, 1, 1))
        one_right = jnp.where(lane == cols - 1, after, pltpu.roll(x, cols - 1, 1))
        return one_left, one_right

    spot = place(offs, lax.axis_index("mode"))
    for c, right, own in ((0, right_0, own_0), (1, right_1, own_1)):
        x = obj[c]
        after = jnp.where(ty == n_ty - 1, 0.0, right[:, 0:1])
        before = jnp.where(ty == 0, 0.0, left[c, :, 127:128])

        def line(rim, flag):
            rim = jnp.where(flag, 0.0, rim)
            whole = jnp.concatenate([rim[k : k + 1, :] for k in range(4)], axis=1)
            return whole, rim[5:6, W - 1 : W], rim[4:5, 0:1]

        u_mid, u_left, u_right = line(up[c], tx == 0)
        d_mid, d_left, d_right = line(down[c], tx == n_tx - 1)
        xl, xr = beside(x, before, after)

        def above(mid, edge):
            return jnp.where(row == 0, edge, pltpu.roll(mid, 1, 0))

        def under(mid, edge):
            return jnp.where(row == W - 1, edge, pltpu.roll(mid, W - 1, 0))

        def shift_line(mid, b, a):
            l1 = lax.broadcasted_iota(jnp.int32, (1, cols), 1)
            return (
                jnp.where(l1 == 0, b, pltpu.roll(mid, 1, 1)),
                jnp.where(l1 == cols - 1, a, pltpu.roll(mid, cols - 1, 1)),
            )

        ul, ur = shift_line(u_mid, u_left, u_right)
        dl, dr = shift_line(d_mid, d_left, d_right)
        xu, xd = above(x, u_mid), under(x, d_mid)
        xul, xur = above(xl, ul), above(xr, ur)
        xdl, xdr = under(xl, dl), under(xr, dr)
        in_col = (lane > 0) | (ty > 0)
        in_row = (row > 0) | (tx > 0)
        total = g[0][0] * x + g[0][1] * xr + g[0][2] * xd + g[0][3] * xdr
        total += jnp.where(in_col, g[1][0] * xl + g[1][1] * x + g[1][2] * xdl + g[1][3] * xd, 0.0)
        total += jnp.where(in_row, g[2][0] * xu + g[2][1] * xur + g[2][2] * x + g[2][3] * xr, 0.0)
        total += jnp.where(
            in_row & in_col, g[3][0] * xul + g[3][1] * xu + g[3][2] * xl + g[3][3] * x, 0.0
        )
        out[c] = x - step_size * total
        take(out, c, own, spot, iota(0) >= spot[0])


def lower_body(one, two, out):
    first = lax.axis_index("ty") == 0
    lane = iota(1)
    total = jnp.zeros((W, W), f32)
    for ref in (one, two):
        keep = (ref[:, W - 1 : W] < 0.5) & (lane < W - 1)
        total = total + jnp.where(keep, ref[...], 0.0)
    out[...] = jnp.where(first, 0.0, total)


def mid_body(offs, above, base, *refs):
    own_p, left_m, left_p, up_m, up_p = (refs[2 * k : 2 * k + 2] for k in range(5))
    out = refs[10]
    m = lax.axis_index("mode")
    tx, ty = lax.axis_index("tx"), lax.axis_index("ty")
    lane, row = iota(1), iota(0)
    out[...] = base[...]
    mine, from_m, from_p = place(offs, 1 - m), place(above, m), place(above, 1 - m)
    for c in range(2):
        for pair in (left_m, left_p):
            ref = pair[c]
            keep = (ref[:, W - 1 : W] > 0.5) & (lane < W - 1) & (ty > 0)
            out[c, :, 0:W] = out[c, :, 0:W] - step_size * jnp.where(keep, ref[...], 0.0)
        take(out, c, own_p[c], mine, row >= mine[0])
        take(out, c, up_m[c], from_m, (row < from_m[0]) & (tx > 0))
        take(out, c, up_p[c], from_p, (row < from_p[0]) & (tx > 0))


def final_body(mid, corner_0, corner_1, out, buf, sems):
    tx = lax.axis_index("tx")
    loads = [pltpu.make_async_copy(mid.at[c, :, 0:W], buf.at[c], sems.at[c]) for c in range(2)]
    stores = [pltpu.make_async_copy(buf.at[c], out.at[c, :, 0:W], sems.at[2 + c]) for c in range(2)]
    for load in loads:
        load.start()
    for c, corner in enumerate((corner_0, corner_1)):
        loads[c].wait()
        buf[c] = buf[c] - step_size * jnp.where(tx > 0, corner[...], 0.0)
        stores[c].start()
    for store in stores:
        store.wait()


def call(body, shapes, in_specs, limit, flops, bytes_accessed, scratch=(), out_spec=VMEM, aliases={}):
    many = isinstance(shapes, list)
    outs = [jax.ShapeDtypeStruct(s, f32) for s in (shapes if many else [shapes])]
    return pl.pallas_call(
        body,
        out_shape=outs if many else outs[0],
        in_specs=in_specs,
        out_specs=[out_spec] * len(outs) if many else out_spec,
        scratch_shapes=list(scratch),
        input_output_aliases=aliases,
        compiler_params=pltpu.CompilerParams(vmem_limit_bytes=limit << 20),
        cost_estimate=pl.CostEstimate(flops=flops, bytes_accessed=bytes_accessed, transcendentals=0),
    )


def local(ring, obj, probe, intensity, offsets, counts, filters):
    def go(value, where):
        return lax.ppermute(value, axes, ring[where])

    tabs = [jnp.asarray(t) for t in tables()]

    rows, cols = obj.shape[1:]
    piece = (W, W)
    whole = (2, rows, cols)
    offs = offsets.reshape(2, 2)
    right = [go(obj[0, :, :W], "left")]
    right.append(go(lax.optimization_barrier(obj)[1, :, :W], "left"))
    core = lax.rem(lax.axis_index("tx"), 2)
    probe_b = go(lax.dynamic_slice_in_dim(probe, core, 1, 0), "swap")
    probe_c = go(probe_b, "core")
    above = go(offs, "down")
    left = go(obj[:, :, cols - 128 :], "right")
    filt = filters.T
    meas = call(sort_body, piece, [VMEM], 8, 1 << 26, 3 << 18)(intensity)
    below = [
        go(
            call(functools.partial(send_body, c), piece, [SMEM] + [VMEM] * 2, 8, 1 << 20, 2 << 20)(
                above, obj, right[c]
            ),
            "up",
        )
        for c in (0, 1)
    ]
    rims = call(rim_body, [(2, 8, W)] * 2, [VMEM] * 4, 8, 1 << 16, 2 << 20)(obj, left, *right)
    under, over = go(rims[0], "up"), go(rims[1], "down")
    g0, g1, s0, s1, k0, k1 = call(
        main_body,
        [piece] * 6,
        [SMEM, SMEM] + [VMEM] * 17,
        16,
        5 << 30,
        12 << 20,
        [pltpu.VMEM((4, 2, W, W), f32)],
    )(offs, counts, obj, *right, *below, probe, probe_b, probe_c, meas, *tabs)
    p1 = go(g1, "swap")
    m0 = go(s0, "right")
    p0 = go(g0, "swap")
    m1 = go(s1, "right")
    b0, b1 = go(g0, "down"), go(g1, "down")
    base = call(prior_body, whole, [SMEM, SMEM] + [VMEM] * 8, 16, 1 << 28, 16 << 20)(
        filt, offs, obj, *right, left, over, under, k0, k1
    )
    n1 = go(call(spill_body, piece, [SMEM, VMEM], 8, 1 << 18, 1 << 19)(offs, p1), "right")
    n0 = go(m0, "swap")
    c1, c0 = go(p1, "down"), go(p0, "down")
    corner = [
        go(call(lower_body, piece, [VMEM] * 2, 8, 1 << 18, 3 << 18)(a, b), "down")
        for a, b in ((m0, n0), (m1, n1))
    ]
    mid = call(mid_body, whole, [SMEM, SMEM] + [VMEM] * 11, 12, 1 << 24, 10 << 20)(
        offs, above, base, p0, p1, m0, m1, n0, n1, b0, b1, c0, c1
    )
    any_space = pl.BlockSpec(memory_space=pl.ANY)
    return call(
        final_body,
        whole,
        [any_space, VMEM, VMEM],
        8,
        1 << 18,
        2 << 20,
        [pltpu.VMEM((2, W, W), f32), pltpu.SemaphoreType.DMA((4,))],
        any_space,
        {0: 0},
    )(mid, *corner)


def solution(mesh):
    placed = (
        P(None, "tx", "ty"),
        P("mode", None, None, None),
        P("tx", "ty", None, None, None),
        P("tx", "ty", None, None),
        P("tx", "ty"),
        P(),
    )

    def body(*args):
        return local(rings(mesh), *args)

    return jax.shard_map(
        body, mesh=mesh, in_specs=placed, out_specs=P(None, "tx", "ty"), check_vma=False
    )
```

```python
import functools
import math

import jax
import jax.numpy as jnp
import numpy as np
from jax import lax
from jax.experimental import pallas as pl
from jax.experimental.pallas import tpu as pltpu
from jax.sharding import PartitionSpec as P


W = 256
axes = ("tx", "ty", "mode")
step_size = 0.25
f32 = jnp.float32
bf16 = jnp.bfloat16
VMEM = pl.BlockSpec(memory_space=pltpu.VMEM)
SMEM = pl.BlockSpec(memory_space=pltpu.SMEM)


def rings(mesh):
    n_tx, n_ty = mesh.shape["tx"], mesh.shape["ty"]
    half = n_ty // 2

    def lin(a, b, m):
        return (a * n_ty + b) * 2 + m

    def perm(move):
        return [
            (lin(a, b, m), lin(*move(a, b, m)))
            for a in range(n_tx)
            for b in range(n_ty)
            for m in range(2)
        ]

    def side(b, d, m):
        other = (b + d) % n_ty
        return other, (1 - m if b // half != other // half else m)

    return {
        "up": perm(lambda a, b, m: ((a - 1) % n_tx, b, m)),
        "down": perm(lambda a, b, m: ((a + 1) % n_tx, b, m)),
        "left": perm(lambda a, b, m: (a, *side(b, -1, m))),
        "right": perm(lambda a, b, m: (a, *side(b, 1, m))),
        "core": perm(lambda a, b, m: (a ^ 1, b, m)),
        "swap": perm(lambda a, b, m: (a, b, 1 - m)),
    }


def split(x):
    high = x.astype(bf16)
    return high, (x - high.astype(f32)).astype(bf16)


def tables():
    half = W // 2
    k, l = np.arange(half)[:, None], np.arange(half)[None, :]
    out = []
    for shift in (0, 1):
        angle = (k * (2 * l + shift) % W) * (2.0 * math.pi / W)
        re, im = np.cos(angle) / math.sqrt(W), -np.sin(angle) / math.sqrt(W)
        block = np.block([[re, im], [-im, re]])
        for mat in (block, block.T):
            high = mat.astype(jnp.bfloat16)
            out += [high, (mat - high.astype(np.float64)).astype(jnp.bfloat16)]
    return out


def dot(a, b):
    return jnp.dot(a, b, preferred_element_type=f32)


def rows_times(x, table):
    xh, xl = split(x)
    high, low = table
    return dot(xh, high) + dot(xh, low) + dot(xl, high)


def cols_times(table, x):
    xh, xl = split(x)
    high, low = table
    return dot(high, xh) + dot(low, xh) + dot(high, xl)


def forward(re, im, even, even_t, odd, odd_t):
    h = W // 2

    def lanes(x, y):
        return jnp.concatenate([x, y], axis=1)

    def stack(x, y):
        return jnp.concatenate([x, y], axis=0)

    e = rows_times(lanes(re[:, :h] + re[:, h:], im[:, :h] + im[:, h:]), even)
    o = rows_times(lanes(re[:, :h] - re[:, h:], im[:, :h] - im[:, h:]), odd)
    re, im = lanes(e[:, :h], o[:, :h]), lanes(e[:, h:], o[:, h:])
    e = cols_times(even_t, stack(re[:h] + re[h:], im[:h] + im[h:]))
    o = cols_times(odd_t, stack(re[:h] - re[h:], im[:h] - im[h:]))
    return stack(e[:h], o[:h]), stack(e[h:], o[h:])


def backward(re, im, even, even_t, odd, odd_t):
    h = W // 2

    def lanes(x, y):
        return jnp.concatenate([x, y], axis=1)

    def stack(x, y):
        return jnp.concatenate([x, y], axis=0)

    a = rows_times(lanes(re[:, :h], im[:, :h]), even_t)
    b = rows_times(lanes(re[:, h:], im[:, h:]), odd_t)
    p, n = a + b, a - b
    re, im = lanes(p[:, :h], n[:, :h]), lanes(p[:, h:], n[:, h:])
    a = cols_times(even, stack(re[:h], im[:h]))
    b = cols_times(odd, stack(re[h:], im[h:]))
    p, n = a + b, a - b
    return stack(p[:h], n[:h]), stack(p[h:], n[h:])


def iota(axis):
    return lax.broadcasted_iota(jnp.int32, (W, W), axis)


def window(obj, c, right, q, s):
    lane = iota(1)
    last = lax.axis_index("ty") == lax.axis_size("ty") - 1
    here = obj[c, :, pl.ds(pl.multiple_of(q * W, W), W)]
    nxt = obj[c, :, pl.ds(pl.multiple_of(jnp.minimum(q + 1, 3) * W, W), W)]
    nxt = jnp.where(q == 3, jnp.where(last, 0.0, right[...]), nxt)
    return jnp.where(lane >= s, here, nxt)


def place(table, slot):
    col0 = table[slot, 1]
    return table[slot, 0], col0 // W, lax.rem(col0, W)


def rim_rows(obj, c, row, right, left):
    last = lax.axis_index("ty") == lax.axis_size("ty") - 1
    first = lax.axis_index("ty") == 0
    edge = jnp.where(first, 0.0, left[c, row : row + 1, :])
    parts = [obj[c, row : row + 1, k * W : (k + 1) * W] for k in range(4)]
    parts.append(jnp.where(last, 0.0, right[row : row + 1, :]))
    parts.append(jnp.concatenate([edge, edge], axis=1))
    return parts


def send_body(c, above, obj, right, out):
    _, q, s = place(above, lax.axis_index("mode"))
    out[...] = window(obj, c, right, q, s)


def rim_body(obj, left, right_0, right_1, up_out, down_out):
    for c, right in enumerate((right_0, right_1)):
        for row, out in ((0, up_out), (W - 1, down_out)):
            for k, part in enumerate(rim_rows(obj, c, row, right, left)):
                out[c, k : k + 1, :] = part
            out[c, 6:8, :] = jnp.zeros((2, W), f32)


def main_body(offs, counts, obj, right_0, right_1, below_0, below_1, probe_a, probe_b, probe_c, meas, *refs):
    mats, (grad_0, grad_1, wave) = refs[:8], refs[8:]
    m = lax.axis_index("mode")
    last_tx = lax.axis_index("tx") == lax.axis_size("tx") - 1
    row0, q, s = place(offs, m)
    live = jnp.where(m < counts[0, 0], 1.0, 0.0).astype(f32)
    lane, row = iota(1), iota(0)
    patch = []
    for c, right, below in ((0, right_0, below_0), (1, right_1, below_1)):
        low = jnp.where(last_tx, 0.0, below[...])
        rolled = jnp.where(row >= row0, window(obj, c, right, q, s), low)
        rolled = pltpu.roll(rolled, lax.rem(W - row0, W), 0)
        patch.append(pltpu.roll(rolled, lax.rem(W - s, W), 1))

    def probe(k, c):
        return (probe_a[0, c], probe_a[1, c], probe_b[0, c], probe_c[0, c])[k]

    tabs = [(mats[2 * k][...], mats[2 * k + 1][...]) for k in range(4)]
    power = jnp.zeros((W, W), f32)
    for k in range(4):
        pr, pi = probe(k, 0), probe(k, 1)
        wr, wi = forward(pr * patch[0] - pi * patch[1], pr * patch[1] + pi * patch[0], *tabs)
        wave[k, 0] = wr
        wave[k, 1] = wi
        power = power + wr * wr + wi * wi
    resid = power - meas[...]
    grad = [jnp.zeros((W, W), f32), jnp.zeros((W, W), f32)]
    for k in range(4):
        pr, pi = probe(k, 0), probe(k, 1)
        br, bi = backward(resid * wave[k, 0], resid * wave[k, 1], *tabs)
        grad[0] = grad[0] + pr * br + pi * bi
        grad[1] = grad[1] + pr * bi - pi * br
    for g, out in ((grad[0], grad_0), (grad[1], grad_1)):
        out[...] = pltpu.roll(pltpu.roll(g * live, row0, 0), s, 1)


def sort_body(meas, out):
    m = lax.axis_index("mode")
    h = W // 2
    lane, row = iota(1), iota(0)

    def nth(k):
        return jnp.where(k < h, 2 * k, 2 * k - W + 1)

    pick_cols = jnp.where(row == nth(lane), 1.0, 0.0).astype(bf16)
    pick_rows = jnp.where(lane == nth(row), 1.0, 0.0).astype(bf16)

    def parts(x):
        for _ in range(3):
            part = x.astype(bf16)
            x = x - part.astype(f32)
            yield part

    x = sum(dot(part, pick_cols) for part in parts(meas[0, 0, m]))
    out[...] = sum(dot(pick_rows, part) for part in parts(x))


def spill_body(n, offs, above, *refs):
    m = lax.axis_index("mode")
    tx = lax.axis_index("tx")
    lane, row = iota(1), iota(0)
    total = jnp.zeros((W, W), f32)
    for k, slot in enumerate((m, 1 - m)[:n]):
        row0, q, s = place(offs, slot)
        total = total + jnp.where((q == 3) & (lane < s) & (row >= row0), refs[k][...], 0.0)
        row0, q, s = place(above, slot)
        keep = (q == 3) & (lane < s) & (row < row0) & (tx > 0)
        total = total + jnp.where(keep, refs[n + k][...], 0.0)
    refs[2 * n][...] = total


def take(out, ref, spot, rows):
    _, q, s = spot
    lane = iota(1)
    value = ref[...]
    here = pl.ds(pl.multiple_of(q * W, W), W)
    out[:, here] = out[:, here] - step_size * jnp.where(rows & (lane >= s), value, 0.0)
    nxt = pl.ds(pl.multiple_of(jnp.minimum(q + 1, 3) * W, W), W)
    keep = rows & (lane < s) & (q < 3)
    out[:, nxt] = out[:, nxt] - step_size * jnp.where(keep, value, 0.0)


def prior_body(c, filt, offs, obj, right, left, up, down, own, out):
    tx, ty = lax.axis_index("tx"), lax.axis_index("ty")
    n_tx, n_ty = lax.axis_size("tx"), lax.axis_size("ty")
    cols = obj.shape[2]
    shape = (W, cols)
    lane = lax.broadcasted_iota(jnp.int32, shape, 1)
    row = lax.broadcasted_iota(jnp.int32, shape, 0)
    taps = [[filt[i, k] for i in range(4)] for k in range(filt.shape[1])]
    g = [[sum(tap[i] * tap[j] for tap in taps) for j in range(4)] for i in range(4)]

    def beside(x, before, after):
        one_left = jnp.where(lane == 0, before, pltpu.roll(x, 1, 1))
        one_right = jnp.where(lane == cols - 1, after, pltpu.roll(x, cols - 1, 1))
        return one_left, one_right

    spot = place(offs, lax.axis_index("mode"))
    x = obj[c]
    after = jnp.where(ty == n_ty - 1, 0.0, right[:, 0:1])
    before = jnp.where(ty == 0, 0.0, left[c, :, 127:128])

    def line(rim, flag):
        rim = jnp.where(flag, 0.0, rim)
        whole = jnp.concatenate([rim[k : k + 1, :] for k in range(4)], axis=1)
        return whole, rim[5:6, W - 1 : W], rim[4:5, 0:1]

    u_mid, u_left, u_right = line(up[c], tx == 0)
    d_mid, d_left, d_right = line(down[c], tx == n_tx - 1)
    xl, xr = beside(x, before, after)

    def above(mid, edge):
        return jnp.where(row == 0, edge, pltpu.roll(mid, 1, 0))

    def under(mid, edge):
        return jnp.where(row == W - 1, edge, pltpu.roll(mid, W - 1, 0))

    def shift_line(mid, b, a):
        l1 = lax.broadcasted_iota(jnp.int32, (1, cols), 1)
        return (
            jnp.where(l1 == 0, b, pltpu.roll(mid, 1, 1)),
            jnp.where(l1 == cols - 1, a, pltpu.roll(mid, cols - 1, 1)),
        )

    ul, ur = shift_line(u_mid, u_left, u_right)
    dl, dr = shift_line(d_mid, d_left, d_right)
    xu, xd = above(x, u_mid), under(x, d_mid)
    xul, xur = above(xl, ul), above(xr, ur)
    xdl, xdr = under(xl, dl), under(xr, dr)
    in_col = (lane > 0) | (ty > 0)
    in_row = (row > 0) | (tx > 0)
    total = g[0][0] * x + g[0][1] * xr + g[0][2] * xd + g[0][3] * xdr
    total += jnp.where(in_col, g[1][0] * xl + g[1][1] * x + g[1][2] * xdl + g[1][3] * xd, 0.0)
    total += jnp.where(in_row, g[2][0] * xu + g[2][1] * xur + g[2][2] * x + g[2][3] * xr, 0.0)
    total += jnp.where(
        in_row & in_col, g[3][0] * xul + g[3][1] * xu + g[3][2] * xl + g[3][3] * x, 0.0
    )
    out[...] = x - step_size * total
    take(out, own, spot, iota(0) >= spot[0])


def mid_body(offs, above, base_0, base_1, own_0, own_1, up_m0, up_m1, up_p0, up_p1, left_0, out, first):
    m = lax.axis_index("mode")
    tx, ty = lax.axis_index("tx"), lax.axis_index("ty")
    row = iota(0)
    mine, from_m, from_p = place(offs, 1 - m), place(above, m), place(above, 1 - m)
    for c, base, own_p, up_m, up_p in (
        (0, base_0, own_0, up_m0, up_p0),
        (1, base_1, own_1, up_m1, up_p1),
    ):
        part = out.at[c]
        part[...] = base[...]
        take(part, own_p, mine, row >= mine[0])
        take(part, up_m, from_m, (row < from_m[0]) & (tx > 0))
        take(part, up_p, from_p, (row < from_p[0]) & (tx > 0))
        value = part[:, 0:W]
        if c == 0:
            value = value - step_size * jnp.where(ty > 0, left_0[...], 0.0)
        first[c] = value


def final_body(mid, first, left_0, left_1, out, buf, sems):
    ty = lax.axis_index("ty")
    stores = [pltpu.make_async_copy(buf.at[c], out.at[c, :, 0:W], sems.at[c]) for c in range(2)]
    for c, left in enumerate((left_0, left_1)):
        buf[c] = first[c] - step_size * jnp.where(ty > 0, left[...], 0.0)
        stores[c].start()
    for store in stores:
        store.wait()


def call(body, shapes, in_specs, limit, flops, bytes_accessed, scratch=(), out_spec=VMEM, aliases={}):
    many = isinstance(shapes, list)
    outs = [jax.ShapeDtypeStruct(s, f32) for s in (shapes if many else [shapes])]
    return pl.pallas_call(
        body,
        out_shape=outs if many else outs[0],
        in_specs=in_specs,
        out_specs=[out_spec] * len(outs) if many else out_spec,
        scratch_shapes=list(scratch),
        input_output_aliases=aliases,
        compiler_params=pltpu.CompilerParams(vmem_limit_bytes=limit << 20),
        cost_estimate=pl.CostEstimate(flops=flops, bytes_accessed=bytes_accessed, transcendentals=0),
    )


def local(ring, obj, probe, intensity, offsets, counts, filters):
    def go(value, where):
        return lax.ppermute(value, axes, ring[where])

    tabs = [jnp.asarray(t) for t in tables()]

    rows, cols = obj.shape[1:]
    piece = (W, W)
    whole = (2, rows, cols)
    offs = offsets.reshape(2, 2)
    right = [go(obj[0, :, :W], "left")]
    right.append(go(lax.optimization_barrier(obj)[1, :, :W], "left"))
    core = lax.rem(lax.axis_index("tx"), 2)
    probe_b = go(lax.dynamic_slice_in_dim(probe, core, 1, 0), "swap")
    probe_c = go(probe_b, "core")
    above = go(offs, "down")
    left = go(obj[:, :, cols - 128 :], "right")
    filt = filters.T
    meas = call(sort_body, piece, [VMEM], 8, 1 << 26, 3 << 18)(intensity)
    below = [
        go(
            call(functools.partial(send_body, c), piece, [SMEM] + [VMEM] * 2, 8, 1 << 20, 2 << 20)(
                above, obj, right[c]
            ),
            "up",
        )
        for c in (0, 1)
    ]
    rims = call(rim_body, [(2, 8, W)] * 2, [VMEM] * 4, 8, 1 << 16, 2 << 20)(obj, left, *right)
    under, over = go(rims[0], "up"), go(rims[1], "down")
    g0, g1 = call(
        main_body,
        [piece] * 2,
        [SMEM, SMEM] + [VMEM] * 17,
        16,
        5 << 30,
        12 << 20,
        [pltpu.VMEM((4, 2, W, W), f32)],
    )(offs, counts, obj, *right, *below, probe, probe_b, probe_c, meas, *tabs)
    p1, b0 = go(g1, "swap"), go(g0, "down")
    p0, b1 = go(g0, "swap"), go(g1, "down")
    base = [
        call(
            functools.partial(prior_body, c), (rows, cols), [SMEM, SMEM] + [VMEM] * 6, 12, 1 << 27, 8 << 20
        )(filt, offs, obj, right[c], left, over, under, g)
        for c, g in ((0, g0), (1, g1))
    ]
    c1, c0 = go(p1, "down"), go(p0, "down")

    def spill(n, *args):
        specs = [SMEM, SMEM] + [VMEM] * (2 * n)
        kernel = call(functools.partial(spill_body, n), piece, specs, 8, 1 << 18, 1 << 20)
        return kernel(offs, above, *args)

    left_m0 = go(spill(1, g0, b0), "right")
    left_p0 = go(left_m0, "swap")
    left_1 = go(spill(2, g1, p1, b1, c1), "right")
    any_space = pl.BlockSpec(memory_space=pl.ANY)
    mid, first = call(
        mid_body, [whole, (2, W, W)], [SMEM, SMEM] + [VMEM] * 9, 12, 1 << 24, 10 << 20
    )(offs, above, *base, p0, p1, b0, b1, c0, c1, left_m0)
    return call(
        final_body,
        whole,
        [any_space] + [VMEM] * 3,
        8,
        1 << 18,
        2 << 20,
        [pltpu.VMEM((2, W, W), f32), pltpu.SemaphoreType.DMA((2,))],
        any_space,
        {0: 0},
    )(mid, first, left_p0, left_1)


def solution(mesh):
    placed = (
        P(None, "tx", "ty"),
        P("mode", None, None, None),
        P("tx", "ty", None, None, None),
        P("tx", "ty", None, None),
        P("tx", "ty"),
        P(),
    )

    def body(*args):
        return local(rings(mesh), *args)

    return jax.shard_map(
        body, mesh=mesh, in_specs=placed, out_specs=P(None, "tx", "ty"), check_vma=False
    )
```

```python
import functools
import math

import jax
import jax.numpy as jnp
import numpy as np
from jax import lax
from jax.experimental import pallas as pl
from jax.experimental.pallas import tpu as pltpu
from jax.sharding import PartitionSpec as P


W = 256
axes = ("tx", "ty", "mode")
step_size = 0.25
f32 = jnp.float32
bf16 = jnp.bfloat16
VMEM = pl.BlockSpec(memory_space=pltpu.VMEM)
SMEM = pl.BlockSpec(memory_space=pltpu.SMEM)


def rings(mesh):
    n_tx, n_ty = mesh.shape["tx"], mesh.shape["ty"]
    half = n_ty // 2

    def lin(a, b, m):
        return (a * n_ty + b) * 2 + m

    def perm(move):
        return [
            (lin(a, b, m), lin(*move(a, b, m)))
            for a in range(n_tx)
            for b in range(n_ty)
            for m in range(2)
        ]

    def side(b, d, m):
        other = (b + d) % n_ty
        return other, (1 - m if b // half != other // half else m)

    return {
        "up": perm(lambda a, b, m: ((a - 1) % n_tx, b, m)),
        "down": perm(lambda a, b, m: ((a + 1) % n_tx, b, m)),
        "left": perm(lambda a, b, m: (a, *side(b, -1, m))),
        "right": perm(lambda a, b, m: (a, *side(b, 1, m))),
        "core": perm(lambda a, b, m: (a ^ 1, b, m)),
        "swap": perm(lambda a, b, m: (a, b, 1 - m)),
    }


def split(x):
    high = x.astype(bf16)
    return high, (x - high.astype(f32)).astype(bf16)


def tables():
    half = W // 2
    k, l = np.arange(half)[:, None], np.arange(half)[None, :]
    out = []
    for shift in (0, 1):
        angle = (k * (2 * l + shift) % W) * (2.0 * math.pi / W)
        re, im = np.cos(angle) / math.sqrt(W), -np.sin(angle) / math.sqrt(W)
        block = np.block([[re, im], [-im, re]])
        for mat in (block, block.T):
            high = mat.astype(jnp.bfloat16)
            out += [high, (mat - high.astype(np.float64)).astype(jnp.bfloat16)]
    return out


def dot(a, b):
    return jnp.dot(a, b, preferred_element_type=f32)


def rows_times(x, table):
    xh, xl = split(x)
    high, low = table
    return dot(xh, high) + dot(xh, low) + dot(xl, high)


def cols_times(table, x):
    xh, xl = split(x)
    high, low = table
    return dot(high, xh) + dot(low, xh) + dot(high, xl)


def forward(re, im, even, even_t, odd, odd_t):
    h = W // 2

    def lanes(x, y):
        return jnp.concatenate([x, y], axis=1)

    def stack(x, y):
        return jnp.concatenate([x, y], axis=0)

    e = rows_times(lanes(re[:, :h] + re[:, h:], im[:, :h] + im[:, h:]), even)
    o = rows_times(lanes(re[:, :h] - re[:, h:], im[:, :h] - im[:, h:]), odd)
    re, im = lanes(e[:, :h], o[:, :h]), lanes(e[:, h:], o[:, h:])
    e = cols_times(even_t, stack(re[:h] + re[h:], im[:h] + im[h:]))
    o = cols_times(odd_t, stack(re[:h] - re[h:], im[:h] - im[h:]))
    return stack(e[:h], o[:h]), stack(e[h:], o[h:])


def backward(re, im, even, even_t, odd, odd_t):
    h = W // 2

    def lanes(x, y):
        return jnp.concatenate([x, y], axis=1)

    def stack(x, y):
        return jnp.concatenate([x, y], axis=0)

    a = rows_times(lanes(re[:, :h], im[:, :h]), even_t)
    b = rows_times(lanes(re[:, h:], im[:, h:]), odd_t)
    p, n = a + b, a - b
    re, im = lanes(p[:, :h], n[:, :h]), lanes(p[:, h:], n[:, h:])
    a = cols_times(even, stack(re[:h], im[:h]))
    b = cols_times(odd, stack(re[h:], im[h:]))
    p, n = a + b, a - b
    return stack(p[:h], n[:h]), stack(p[h:], n[h:])


def iota(axis):
    return lax.broadcasted_iota(jnp.int32, (W, W), axis)


def window(obj, c, right, q, s):
    lane = iota(1)
    last = lax.axis_index("ty") == lax.axis_size("ty") - 1
    here = obj[c, :, pl.ds(pl.multiple_of(q * W, W), W)]
    nxt = obj[c, :, pl.ds(pl.multiple_of(jnp.minimum(q + 1, 3) * W, W), W)]
    nxt = jnp.where(q == 3, jnp.where(last, 0.0, right[...]), nxt)
    return jnp.where(lane >= s, here, nxt)


def place(table, slot):
    col0 = table[slot, 1]
    return table[slot, 0], col0 // W, lax.rem(col0, W)


def rim_rows(out, at, obj, c, row, right, left):
    last = lax.axis_index("ty") == lax.axis_size("ty") - 1
    first = lax.axis_index("ty") == 0
    for k in range(4):
        out[at + k : at + k + 1, :] = obj[c, row : row + 1, k * W : (k + 1) * W]
    out[at + 4 : at + 5, :] = jnp.where(last, 0.0, right[row : row + 1, :])
    out[at + 5 : at + 6, :] = jnp.where(first, 0.0, left[c : c + 1, :])
    out[at + 6 : at + 8, :] = jnp.zeros((2, W), f32)


def edge_body(obj, out):
    cols = obj.shape[2]
    for c in range(2):
        out[c : c + 1, :] = obj[c, :, cols - 128 : cols].T[127:128, :]
    out[2:8, :] = jnp.zeros((6, W), f32)


def send_body(c, above, obj, *refs):
    _, q, s = place(above, lax.axis_index("mode"))
    out = refs[-1]
    out[0:W, :] = window(obj, c, refs[c], q, s)
    if c == 1:
        for d in range(2):
            rim_rows(out, W + 8 * d, obj, d, 0, refs[d], refs[2])


def main_body(offs, counts, obj, left, right_0, right_1, below_0, below_1, probe_a, probe_b, probe_c, meas, *refs):
    mats, (grad_0, grad_1, wave) = refs[:8], refs[8:]
    m = lax.axis_index("mode")
    last_tx = lax.axis_index("tx") == lax.axis_size("tx") - 1
    row0, q, s = place(offs, m)
    live = jnp.where(m < counts[0, 0], 1.0, 0.0).astype(f32)
    lane, row = iota(1), iota(0)
    patch = []
    for c, right, below in ((0, right_0, below_0), (1, right_1, below_1)):
        low = jnp.where(last_tx, 0.0, below[0:W, :])
        rolled = jnp.where(row >= row0, window(obj, c, right, q, s), low)
        rolled = pltpu.roll(rolled, lax.rem(W - row0, W), 0)
        patch.append(pltpu.roll(rolled, lax.rem(W - s, W), 1))

    def probe(k, c):
        return (probe_a[0, c], probe_a[1, c], probe_b[0, c], probe_c[0, c])[k]

    tabs = [(mats[2 * k][...], mats[2 * k + 1][...]) for k in range(4)]
    power = jnp.zeros((W, W), f32)
    for k in range(4):
        pr, pi = probe(k, 0), probe(k, 1)
        wr, wi = forward(pr * patch[0] - pi * patch[1], pr * patch[1] + pi * patch[0], *tabs)
        wave[k, 0] = wr
        wave[k, 1] = wi
        power = power + wr * wr + wi * wi
    resid = power - meas[...]
    grad = [jnp.zeros((W, W), f32), jnp.zeros((W, W), f32)]
    for k in range(4):
        pr, pi = probe(k, 0), probe(k, 1)
        br, bi = backward(resid * wave[k, 0], resid * wave[k, 1], *tabs)
        grad[0] = grad[0] + pr * br + pi * bi
        grad[1] = grad[1] + pr * bi - pi * br
    for c, right, out in ((0, right_0, grad_0), (1, right_1, grad_1)):
        out[0:W, :] = pltpu.roll(pltpu.roll(grad[c] * live, row0, 0), s, 1)
        rim_rows(out, W, obj, c, W - 1, right, left)


def sort_body(meas, out):
    m = lax.axis_index("mode")
    h = W // 2
    lane, row = iota(1), iota(0)

    def nth(k):
        return jnp.where(k < h, 2 * k, 2 * k - W + 1)

    pick_cols = jnp.where(row == nth(lane), 1.0, 0.0).astype(bf16)
    pick_rows = jnp.where(lane == nth(row), 1.0, 0.0).astype(bf16)

    def parts(x):
        for _ in range(3):
            part = x.astype(bf16)
            x = x - part.astype(f32)
            yield part

    x = sum(dot(part, pick_cols) for part in parts(meas[0, 0, m]))
    out[...] = sum(dot(pick_rows, part) for part in parts(x))


def spill_body(n, offs, above, *refs):
    m = lax.axis_index("mode")
    tx = lax.axis_index("tx")
    lane, row = iota(1), iota(0)
    total = jnp.zeros((W, W), f32)
    for k, slot in enumerate((m, 1 - m)[:n]):
        row0, q, s = place(offs, slot)
        total = total + jnp.where((q == 3) & (lane < s) & (row >= row0), refs[k][0:W, :], 0.0)
        row0, q, s = place(above, slot)
        keep = (q == 3) & (lane < s) & (row < row0) & (tx > 0)
        total = total + jnp.where(keep, refs[n + k][0:W, :], 0.0)
    refs[2 * n][...] = total


def take(out, ref, spot, rows):
    _, q, s = spot
    lane = iota(1)
    value = ref[0:W, :]
    here = pl.ds(pl.multiple_of(q * W, W), W)
    out[:, here] = out[:, here] - step_size * jnp.where(rows & (lane >= s), value, 0.0)
    nxt = pl.ds(pl.multiple_of(jnp.minimum(q + 1, 3) * W, W), W)
    keep = rows & (lane < s) & (q < 3)
    out[:, nxt] = out[:, nxt] - step_size * jnp.where(keep, value, 0.0)


def prior_body(c, filt, offs, above, obj, right, left, up, down, own, out):
    tx, ty = lax.axis_index("tx"), lax.axis_index("ty")
    n_tx, n_ty = lax.axis_size("tx"), lax.axis_size("ty")
    cols = obj.shape[2]
    shape = (W, cols)
    lane = lax.broadcasted_iota(jnp.int32, shape, 1)
    row = lax.broadcasted_iota(jnp.int32, shape, 0)
    taps = [[filt[i, k] for i in range(4)] for k in range(filt.shape[1])]
    g = [[sum(tap[i] * tap[j] for tap in taps) for j in range(4)] for i in range(4)]

    def beside(x, before, after):
        one_left = jnp.where(lane == 0, before, pltpu.roll(x, 1, 1))
        one_right = jnp.where(lane == cols - 1, after, pltpu.roll(x, cols - 1, 1))
        return one_left, one_right

    spot = place(offs, lax.axis_index("mode"))
    x = obj[c]
    after = jnp.where(ty == n_ty - 1, 0.0, right[:, 0:1])
    edge = jnp.broadcast_to(left[c : c + 1, :], (128, W)).T
    before = jnp.where(ty == 0, 0.0, edge[:, 0:1])

    def line(rim, flag, at):
        rim = jnp.where(flag, 0.0, rim)
        whole = jnp.concatenate([rim[k : k + 1, :] for k in range(4)], axis=1)
        return whole, rim[5:6, at : at + 1], rim[4:5, 0:1]

    u_mid, u_left, u_right = line(up[W : W + 8, :], tx == 0, W - 1)
    d_mid, d_left, d_right = line(down[W + 8 * c : W + 8 * c + 8, :], tx == n_tx - 1, 0)
    xl, xr = beside(x, before, after)

    def over(mid, edge):
        return jnp.where(row == 0, edge, pltpu.roll(mid, 1, 0))

    def under(mid, edge):
        return jnp.where(row == W - 1, edge, pltpu.roll(mid, W - 1, 0))

    def shift_line(mid, b, a):
        l1 = lax.broadcasted_iota(jnp.int32, (1, cols), 1)
        return (
            jnp.where(l1 == 0, b, pltpu.roll(mid, 1, 1)),
            jnp.where(l1 == cols - 1, a, pltpu.roll(mid, cols - 1, 1)),
        )

    ul, ur = shift_line(u_mid, u_left, u_right)
    dl, dr = shift_line(d_mid, d_left, d_right)
    xu, xd = over(x, u_mid), under(x, d_mid)
    xul, xur = over(xl, ul), over(xr, ur)
    xdl, xdr = under(xl, dl), under(xr, dr)
    in_col = (lane > 0) | (ty > 0)
    in_row = (row > 0) | (tx > 0)
    total = g[0][0] * x + g[0][1] * xr + g[0][2] * xd + g[0][3] * xdr
    total += jnp.where(in_col, g[1][0] * xl + g[1][1] * x + g[1][2] * xdl + g[1][3] * xd, 0.0)
    total += jnp.where(in_row, g[2][0] * xu + g[2][1] * xur + g[2][2] * x + g[2][3] * xr, 0.0)
    total += jnp.where(
        in_row & in_col, g[3][0] * xul + g[3][1] * xu + g[3][2] * xl + g[3][3] * x, 0.0
    )
    out[...] = x - step_size * total
    take(out, own, spot, iota(0) >= spot[0])
    spot = place(above, lax.axis_index("mode"))
    take(out, up, spot, (iota(0) < spot[0]) & (tx > 0))


def fold_body(offs, above, base, own_p, up_p, out):
    slot = 1 - lax.axis_index("mode")
    row = iota(0)
    mine, over = place(offs, slot), place(above, slot)
    out[...] = base[...]
    take(out, own_p, mine, row >= mine[0])
    take(out, up_p, over, (row < over[0]) & (lax.axis_index("tx") > 0))


def mid_body(offs, above, base, own_p, up_p, left_0, done, out, first):
    part = out.at[0]
    fold_body(offs, above, base, own_p, up_p, part)
    first[0] = part[:, 0:W] - step_size * jnp.where(lax.axis_index("ty") > 0, left_0[...], 0.0)
    out[1] = done[...]
    first[1] = done[:, 0:W]


def final_body(mid, first, left_0, left_1, out, buf, sems):
    ty = lax.axis_index("ty")
    stores = [pltpu.make_async_copy(buf.at[c], out.at[c, :, 0:W], sems.at[c]) for c in range(2)]
    for c, left in enumerate((left_0, left_1)):
        buf[c] = first[c] - step_size * jnp.where(ty > 0, left[...], 0.0)
        stores[c].start()
    for store in stores:
        store.wait()


def call(body, shapes, in_specs, limit, flops, bytes_accessed, scratch=(), out_spec=VMEM, aliases={}):
    many = isinstance(shapes, list)
    outs = [jax.ShapeDtypeStruct(s, f32) for s in (shapes if many else [shapes])]
    return pl.pallas_call(
        body,
        out_shape=outs if many else outs[0],
        in_specs=in_specs,
        out_specs=[out_spec] * len(outs) if many else out_spec,
        scratch_shapes=list(scratch),
        input_output_aliases=aliases,
        compiler_params=pltpu.CompilerParams(vmem_limit_bytes=limit << 20),
        cost_estimate=pl.CostEstimate(flops=flops, bytes_accessed=bytes_accessed, transcendentals=0),
    )


def local(ring, obj, probe, intensity, offsets, counts, filters):
    def go(value, where):
        return lax.ppermute(value, axes, ring[where])

    tabs = [jnp.asarray(t) for t in tables()]

    rows, cols = obj.shape[1:]
    piece = (W, W)
    whole = (2, rows, cols)
    offs = offsets.reshape(2, 2)
    right = [go(obj[0, :, :W], "left")]
    right.append(go(lax.optimization_barrier(obj)[1, :, :W], "left"))
    core = lax.rem(lax.axis_index("tx"), 2)
    probe_b = go(lax.dynamic_slice_in_dim(probe, core, 1, 0), "swap")
    probe_c = go(probe_b, "core")
    above = go(offs, "down")
    edge = call(edge_body, (8, W), [VMEM], 8, 1 << 16, 1 << 18)(obj)
    left = go(edge, "right")
    filt = filters.T
    meas = call(sort_body, piece, [VMEM], 8, 1 << 26, 3 << 18)(intensity)
    up_0 = call(
        functools.partial(send_body, 0), piece, [SMEM] + [VMEM] * 2, 8, 1 << 20, 2 << 20
    )(above, obj, right[0])
    below_0 = go(up_0, "up")
    up_1 = call(
        functools.partial(send_body, 1), (W + 16, W), [SMEM] + [VMEM] * 4, 8, 1 << 20, 2 << 20
    )(above, obj, *right, left)
    below_1 = go(up_1, "up")
    g0, g1 = call(
        main_body,
        [(W + 8, W)] * 2,
        [SMEM, SMEM] + [VMEM] * 18,
        16,
        5 << 30,
        12 << 20,
        [pltpu.VMEM((4, 2, W, W), f32)],
    )(offs, counts, obj, left, *right, below_0, below_1, probe, probe_b, probe_c, meas, *tabs)
    p1, b0 = go(g1, "swap"), go(g0, "down")
    p0, b1 = go(g0, "swap"), go(g1, "down")
    base = [
        call(
            functools.partial(prior_body, c), (rows, cols), [SMEM] * 3 + [VMEM] * 6, 12, 1 << 27, 8 << 20
        )(filt, offs, above, obj, right[c], left, b, below_1, g)
        for c, g, b in ((0, g0, b0), (1, g1, b1))
    ]
    c1, c0 = go(p1, "down"), go(p0, "down")

    def spill(n, *args):
        specs = [SMEM, SMEM] + [VMEM] * (2 * n)
        kernel = call(functools.partial(spill_body, n), piece, specs, 8, 1 << 18, 1 << 20)
        return kernel(offs, above, *args)

    left_m0 = go(spill(1, g0, b0), "right")
    left_p0 = go(left_m0, "swap")
    left_1 = go(spill(2, g1, p1, b1, c1), "right")
    any_space = pl.BlockSpec(memory_space=pl.ANY)
    fold = call(fold_body, (rows, cols), [SMEM, SMEM] + [VMEM] * 3, 8, 1 << 20, 4 << 20)(
        offs, above, base[1], p1, c1
    )
    mid, first = call(
        mid_body, [whole, (2, W, W)], [SMEM, SMEM] + [VMEM] * 5, 12, 1 << 24, 10 << 20
    )(offs, above, base[0], p0, c0, left_m0, fold)
    return call(
        final_body,
        whole,
        [any_space] + [VMEM] * 3,
        8,
        1 << 18,
        2 << 20,
        [pltpu.VMEM((2, W, W), f32), pltpu.SemaphoreType.DMA((2,))],
        any_space,
        {0: 0},
    )(mid, first, left_p0, left_1)


def solution(mesh):
    placed = (
        P(None, "tx", "ty"),
        P("mode", None, None, None),
        P("tx", "ty", None, None, None),
        P("tx", "ty", None, None),
        P("tx", "ty"),
        P(),
    )

    def body(*args):
        return local(rings(mesh), *args)

    return jax.shard_map(
        body, mesh=mesh, in_specs=placed, out_specs=P(None, "tx", "ty"), check_vma=False
    )
```

```python
import functools
import math

import jax
import jax.numpy as jnp
import numpy as np
from jax import lax
from jax.experimental import pallas as pl
from jax.experimental.pallas import tpu as pltpu
from jax.sharding import PartitionSpec as P


W = 256
axes = ("tx", "ty", "mode")
step_size = 0.25
f32 = jnp.float32
bf16 = jnp.bfloat16
VMEM = pl.BlockSpec(memory_space=pltpu.VMEM)
SMEM = pl.BlockSpec(memory_space=pltpu.SMEM)


def rings(mesh):
    n_tx, n_ty = mesh.shape["tx"], mesh.shape["ty"]
    half = n_ty // 2

    def lin(a, b, m):
        return (a * n_ty + b) * 2 + m

    def perm(move):
        return [
            (lin(a, b, m), lin(*move(a, b, m)))
            for a in range(n_tx)
            for b in range(n_ty)
            for m in range(2)
        ]

    def side(b, d, m):
        other = (b + d) % n_ty
        return other, (1 - m if b // half != other // half else m)

    return {
        "up": perm(lambda a, b, m: ((a - 1) % n_tx, b, m)),
        "down": perm(lambda a, b, m: ((a + 1) % n_tx, b, m)),
        "left": perm(lambda a, b, m: (a, *side(b, -1, m))),
        "right": perm(lambda a, b, m: (a, *side(b, 1, m))),
        "core": perm(lambda a, b, m: (a ^ 1, b, m)),
        "swap": perm(lambda a, b, m: (a, b, 1 - m)),
    }


def split(x):
    high = x.astype(bf16)
    return high, (x - high.astype(f32)).astype(bf16)


def tables():
    half = W // 2
    k, l = np.arange(half)[:, None], np.arange(half)[None, :]
    out = []
    for shift in (0, 1):
        angle = (k * (2 * l + shift) % W) * (2.0 * math.pi / W)
        re, im = np.cos(angle) / math.sqrt(W), -np.sin(angle) / math.sqrt(W)
        block = np.block([[re, im], [-im, re]])
        for mat in (block, block.T):
            high = mat.astype(jnp.bfloat16)
            out += [high, (mat - high.astype(np.float64)).astype(jnp.bfloat16)]
    return out


def dot(a, b):
    return jnp.dot(a, b, preferred_element_type=f32)


def rows_times(x, table):
    xh, xl = split(x)
    high, low = table
    return dot(xh, high) + dot(xh, low) + dot(xl, high)


def cols_times(table, x):
    xh, xl = split(x)
    high, low = table
    return dot(high, xh) + dot(low, xh) + dot(high, xl)


def forward(re, im, even, even_t, odd, odd_t):
    h = W // 2

    def lanes(x, y):
        return jnp.concatenate([x, y], axis=1)

    def stack(x, y):
        return jnp.concatenate([x, y], axis=0)

    e = rows_times(lanes(re[:, :h] + re[:, h:], im[:, :h] + im[:, h:]), even)
    o = rows_times(lanes(re[:, :h] - re[:, h:], im[:, :h] - im[:, h:]), odd)
    re, im = lanes(e[:, :h], o[:, :h]), lanes(e[:, h:], o[:, h:])
    e = cols_times(even_t, stack(re[:h] + re[h:], im[:h] + im[h:]))
    o = cols_times(odd_t, stack(re[:h] - re[h:], im[:h] - im[h:]))
    return stack(e[:h], o[:h]), stack(e[h:], o[h:])


def backward(re, im, even, even_t, odd, odd_t):
    h = W // 2

    def lanes(x, y):
        return jnp.concatenate([x, y], axis=1)

    def stack(x, y):
        return jnp.concatenate([x, y], axis=0)

    a = rows_times(lanes(re[:, :h], im[:, :h]), even_t)
    b = rows_times(lanes(re[:, h:], im[:, h:]), odd_t)
    p, n = a + b, a - b
    re, im = lanes(p[:, :h], n[:, :h]), lanes(p[:, h:], n[:, h:])
    a = cols_times(even, stack(re[:h], im[:h]))
    b = cols_times(odd, stack(re[h:], im[h:]))
    p, n = a + b, a - b
    return stack(p[:h], n[:h]), stack(p[h:], n[h:])


def iota(axis):
    return lax.broadcasted_iota(jnp.int32, (W, W), axis)


def window(obj, c, right, q, s):
    lane = iota(1)
    last = lax.axis_index("ty") == lax.axis_size("ty") - 1
    here = obj[c, :, pl.ds(pl.multiple_of(q * W, W), W)]
    nxt = obj[c, :, pl.ds(pl.multiple_of(jnp.minimum(q + 1, 3) * W, W), W)]
    nxt = jnp.where(q == 3, jnp.where(last, 0.0, right[...]), nxt)
    return jnp.where(lane >= s, here, nxt)


def place(table, slot):
    col0 = table[slot, 1]
    return table[slot, 0], col0 // W, lax.rem(col0, W)


def rim_rows(out, at, obj, c, row, right, left):
    last = lax.axis_index("ty") == lax.axis_size("ty") - 1
    first = lax.axis_index("ty") == 0
    for k in range(4):
        out[at + k : at + k + 1, :] = obj[c, row : row + 1, k * W : (k + 1) * W]
    out[at + 4 : at + 5, :] = jnp.where(last, 0.0, right[row : row + 1, :])
    out[at + 5 : at + 6, :] = jnp.where(first, 0.0, left[c : c + 1, :])
    out[at + 6 : at + 8, :] = jnp.zeros((2, W), f32)


def edge_body(obj, out):
    cols = obj.shape[2]
    for c in range(2):
        out[c : c + 1, :] = obj[c, :, cols - 128 : cols].T[127:128, :]
    out[2:8, :] = jnp.zeros((6, W), f32)


def send_body(c, above, obj, *refs):
    _, q, s = place(above, lax.axis_index("mode"))
    out = refs[c + 1 + c]
    out[0:W, :] = window(obj, c, refs[c], q, s)
    if c == 1:
        for d in range(2):
            rim_rows(out, W + 8 * d, obj, d, 0, refs[d], refs[2])
            rim_rows(refs[4], 8 * d, obj, d, W - 1, refs[d], refs[2])


def main_body(offs, counts, obj, right_0, right_1, below_0, below_1, probe_a, probe_b, probe_c, meas, *refs):
    mats, (grad_0, grad_1, wave) = refs[:8], refs[8:]
    m = lax.axis_index("mode")
    last_tx = lax.axis_index("tx") == lax.axis_size("tx") - 1
    row0, q, s = place(offs, m)
    live = jnp.where(m < counts[0, 0], 1.0, 0.0).astype(f32)
    lane, row = iota(1), iota(0)
    patch = []
    for c, right, below in ((0, right_0, below_0), (1, right_1, below_1)):
        low = jnp.where(last_tx, 0.0, below[0:W, :])
        rolled = jnp.where(row >= row0, window(obj, c, right, q, s), low)
        rolled = pltpu.roll(rolled, lax.rem(W - row0, W), 0)
        patch.append(pltpu.roll(rolled, lax.rem(W - s, W), 1))

    def probe(k, c):
        return (probe_a[0, c], probe_a[1, c], probe_b[0, c], probe_c[0, c])[k]

    tabs = [(mats[2 * k][...], mats[2 * k + 1][...]) for k in range(4)]
    power = jnp.zeros((W, W), f32)
    for k in range(4):
        pr, pi = probe(k, 0), probe(k, 1)
        wr, wi = forward(pr * patch[0] - pi * patch[1], pr * patch[1] + pi * patch[0], *tabs)
        wave[k, 0] = wr
        wave[k, 1] = wi
        power = power + wr * wr + wi * wi
    resid = power - meas[...]
    grad = [jnp.zeros((W, W), f32), jnp.zeros((W, W), f32)]
    for k in range(4):
        pr, pi = probe(k, 0), probe(k, 1)
        br, bi = backward(resid * wave[k, 0], resid * wave[k, 1], *tabs)
        grad[0] = grad[0] + pr * br + pi * bi
        grad[1] = grad[1] + pr * bi - pi * br
    for g, out in ((grad[0], grad_0), (grad[1], grad_1)):
        out[...] = pltpu.roll(pltpu.roll(g * live, row0, 0), s, 1)


def sort_body(meas, out):
    m = lax.axis_index("mode")
    h = W // 2
    lane, row = iota(1), iota(0)

    def nth(k):
        return jnp.where(k < h, 2 * k, 2 * k - W + 1)

    pick_cols = jnp.where(row == nth(lane), 1.0, 0.0).astype(bf16)
    pick_rows = jnp.where(lane == nth(row), 1.0, 0.0).astype(bf16)

    def parts(x):
        for _ in range(3):
            part = x.astype(bf16)
            x = x - part.astype(f32)
            yield part

    x = sum(dot(part, pick_cols) for part in parts(meas[0, 0, m]))
    out[...] = sum(dot(pick_rows, part) for part in parts(x))


def spill_body(n, offs, above, *refs):
    m = lax.axis_index("mode")
    tx = lax.axis_index("tx")
    lane, row = iota(1), iota(0)
    total = jnp.zeros((W, W), f32)
    for k, slot in enumerate((m, 1 - m)[:n]):
        row0, q, s = place(offs, slot)
        total = total + jnp.where((q == 3) & (lane < s) & (row >= row0), refs[k][...], 0.0)
        row0, q, s = place(above, slot)
        keep = (q == 3) & (lane < s) & (row < row0) & (tx > 0)
        total = total + jnp.where(keep, refs[n + k][...], 0.0)
    refs[2 * n][...] = total


def take(out, ref, spot, rows):
    _, q, s = spot
    lane = iota(1)
    value = ref[...]
    here = pl.ds(pl.multiple_of(q * W, W), W)
    out[:, here] = out[:, here] - step_size * jnp.where(rows & (lane >= s), value, 0.0)
    nxt = pl.ds(pl.multiple_of(jnp.minimum(q + 1, 3) * W, W), W)
    keep = rows & (lane < s) & (q < 3)
    out[:, nxt] = out[:, nxt] - step_size * jnp.where(keep, value, 0.0)


def take_all(out, offs, above, refs, skip=0):
    m = lax.axis_index("mode")
    row = iota(0)
    n = len(refs) // 2
    for k, slot in enumerate((m, 1 - m)[skip : skip + n]):
        spot = place(offs, slot)
        take(out, refs[k], spot, row >= spot[0])
        spot = place(above, slot)
        take(out, refs[n + k], spot, (row < spot[0]) & (lax.axis_index("tx") > 0))


def prior_body(c, filt, offs, above, obj, right, left, up, down, *refs):
    out = refs[-1]
    tx, ty = lax.axis_index("tx"), lax.axis_index("ty")
    n_tx, n_ty = lax.axis_size("tx"), lax.axis_size("ty")
    cols = obj.shape[2]
    shape = (W, cols)
    lane = lax.broadcasted_iota(jnp.int32, shape, 1)
    row = lax.broadcasted_iota(jnp.int32, shape, 0)
    taps = [[filt[i, k] for i in range(4)] for k in range(filt.shape[1])]
    g = [[sum(tap[i] * tap[j] for tap in taps) for j in range(4)] for i in range(4)]

    def beside(x, before, after):
        one_left = jnp.where(lane == 0, before, pltpu.roll(x, 1, 1))
        one_right = jnp.where(lane == cols - 1, after, pltpu.roll(x, cols - 1, 1))
        return one_left, one_right

    x = obj[c]
    after = jnp.where(ty == n_ty - 1, 0.0, right[:, 0:1])
    edge = jnp.broadcast_to(left[c : c + 1, :], (128, W)).T
    before = jnp.where(ty == 0, 0.0, edge[:, 0:1])

    def line(rim, flag, at):
        rim = jnp.where(flag, 0.0, rim)
        whole = jnp.concatenate([rim[k : k + 1, :] for k in range(4)], axis=1)
        return whole, rim[5:6, at : at + 1], rim[4:5, 0:1]

    u_mid, u_left, u_right = line(up[8 * c : 8 * c + 8, :], tx == 0, W - 1)
    d_mid, d_left, d_right = line(down[W + 8 * c : W + 8 * c + 8, :], tx == n_tx - 1, 0)
    xl, xr = beside(x, before, after)

    def over(mid, edge):
        return jnp.where(row == 0, edge, pltpu.roll(mid, 1, 0))

    def under(mid, edge):
        return jnp.where(row == W - 1, edge, pltpu.roll(mid, W - 1, 0))

    def shift_line(mid, b, a):
        l1 = lax.broadcasted_iota(jnp.int32, (1, cols), 1)
        return (
            jnp.where(l1 == 0, b, pltpu.roll(mid, 1, 1)),
            jnp.where(l1 == cols - 1, a, pltpu.roll(mid, cols - 1, 1)),
        )

    ul, ur = shift_line(u_mid, u_left, u_right)
    dl, dr = shift_line(d_mid, d_left, d_right)
    xu, xd = over(x, u_mid), under(x, d_mid)
    xul, xur = over(xl, ul), over(xr, ur)
    xdl, xdr = under(xl, dl), under(xr, dr)
    in_col = (lane > 0) | (ty > 0)
    in_row = (row > 0) | (tx > 0)
    total = g[0][0] * x + g[0][1] * xr + g[0][2] * xd + g[0][3] * xdr
    total += jnp.where(in_col, g[1][0] * xl + g[1][1] * x + g[1][2] * xdl + g[1][3] * xd, 0.0)
    total += jnp.where(in_row, g[2][0] * xu + g[2][1] * xur + g[2][2] * x + g[2][3] * xr, 0.0)
    total += jnp.where(
        in_row & in_col, g[3][0] * xul + g[3][1] * xu + g[3][2] * xl + g[3][3] * x, 0.0
    )
    out[...] = x - step_size * total
    take_all(out, offs, above, refs[:-1])


def mid_body(offs, above, base, own_p, up_p, left_0, done, out, first):
    part = out.at[0]
    part[...] = base[...]
    take_all(part, offs, above, (own_p, up_p), 1)
    first[0] = part[:, 0:W] - step_size * jnp.where(lax.axis_index("ty") > 0, left_0[...], 0.0)
    out[1] = done[...]
    first[1] = done[:, 0:W]


def final_body(mid, first, left_0, left_1, out, buf, sems):
    ty = lax.axis_index("ty")
    stores = [pltpu.make_async_copy(buf.at[c], out.at[c, :, 0:W], sems.at[c]) for c in range(2)]
    for c, left in enumerate((left_0, left_1)):
        buf[c] = first[c] - step_size * jnp.where(ty > 0, left[...], 0.0)
        stores[c].start()
    for store in stores:
        store.wait()


def call(body, shapes, in_specs, limit, flops, bytes_accessed, scratch=(), out_spec=VMEM, aliases={}):
    many = isinstance(shapes, list)
    outs = [jax.ShapeDtypeStruct(s, f32) for s in (shapes if many else [shapes])]
    return pl.pallas_call(
        body,
        out_shape=outs if many else outs[0],
        in_specs=in_specs,
        out_specs=[out_spec] * len(outs) if many else out_spec,
        scratch_shapes=list(scratch),
        input_output_aliases=aliases,
        compiler_params=pltpu.CompilerParams(vmem_limit_bytes=limit << 20),
        cost_estimate=pl.CostEstimate(flops=flops, bytes_accessed=bytes_accessed, transcendentals=0),
    )


def local(ring, obj, probe, intensity, offsets, counts, filters):
    def go(value, where):
        return lax.ppermute(value, axes, ring[where])

    tabs = [jnp.asarray(t) for t in tables()]

    rows, cols = obj.shape[1:]
    piece = (W, W)
    whole = (2, rows, cols)
    offs = offsets.reshape(2, 2)
    right = [go(obj[0, :, :W], "left")]
    right.append(go(lax.optimization_barrier(obj)[1, :, :W], "left"))
    core = lax.rem(lax.axis_index("tx"), 2)
    probe_b = go(lax.dynamic_slice_in_dim(probe, core, 1, 0), "swap")
    probe_c = go(probe_b, "core")
    above = go(offs, "down")
    edge = call(edge_body, (8, W), [VMEM], 8, 1 << 16, 1 << 18)(obj)
    left = go(edge, "right")
    filt = filters.T
    meas = call(sort_body, piece, [VMEM], 8, 1 << 26, 3 << 18)(intensity)
    up_0 = call(
        functools.partial(send_body, 0), piece, [SMEM] + [VMEM] * 2, 8, 1 << 20, 2 << 20
    )(above, obj, right[0])
    below_0 = go(up_0, "up")
    up_1, rim = call(
        functools.partial(send_body, 1),
        [(W + 16, W), (16, W)],
        [SMEM] + [VMEM] * 4,
        8,
        1 << 20,
        2 << 20,
    )(above, obj, *right, left)
    below_1 = go(up_1, "up")
    over = go(rim, "down")
    g0, g1 = call(
        main_body,
        [piece] * 2,
        [SMEM, SMEM] + [VMEM] * 17,
        16,
        5 << 30,
        12 << 20,
        [pltpu.VMEM((4, 2, W, W), f32)],
    )(offs, counts, obj, *right, below_0, below_1, probe, probe_b, probe_c, meas, *tabs)
    p1, b0 = go(g1, "swap"), go(g0, "down")
    p0, b1 = go(g0, "swap"), go(g1, "down")
    c1, c0 = go(p1, "down"), go(p0, "down")

    def prior(c, *args):
        specs = [SMEM] * 3 + [VMEM] * (5 + len(args))
        kernel = call(functools.partial(prior_body, c), (rows, cols), specs, 12, 1 << 27, 8 << 20)
        return kernel(filt, offs, above, obj, right[c], left, over, below_1, *args)

    base = [prior(0, g0, b0), prior(1, g1, p1, b1, c1)]

    def spill(n, *args):
        specs = [SMEM, SMEM] + [VMEM] * (2 * n)
        kernel = call(functools.partial(spill_body, n), piece, specs, 8, 1 << 18, 1 << 20)
        return kernel(offs, above, *args)

    left_m0 = go(spill(1, g0, b0), "right")
    left_p0 = go(left_m0, "swap")
    left_1 = go(spill(2, g1, p1, b1, c1), "right")
    any_space = pl.BlockSpec(memory_space=pl.ANY)
    mid, first = call(
        mid_body, [whole, (2, W, W)], [SMEM, SMEM] + [VMEM] * 5, 12, 1 << 24, 10 << 20
    )(offs, above, base[0], p0, c0, left_m0, base[1])
    return call(
        final_body,
        whole,
        [any_space] + [VMEM] * 3,
        8,
        1 << 18,
        2 << 20,
        [pltpu.VMEM((2, W, W), f32), pltpu.SemaphoreType.DMA((2,))],
        any_space,
        {0: 0},
    )(mid, first, left_p0, left_1)


def solution(mesh):
    placed = (
        P(None, "tx", "ty"),
        P("mode", None, None, None),
        P("tx", "ty", None, None, None),
        P("tx", "ty", None, None),
        P("tx", "ty"),
        P(),
    )

    def body(*args):
        return local(rings(mesh), *args)

    return jax.shard_map(
        body, mesh=mesh, in_specs=placed, out_specs=P(None, "tx", "ty"), check_vma=False
    )
```

```python
import functools
import math

import jax
import jax.numpy as jnp
import numpy as np
from jax import lax
from jax.experimental import pallas as pl
from jax.experimental.pallas import tpu as pltpu
from jax.sharding import PartitionSpec as P


W = 256
axes = ("tx", "ty", "mode")
step_size = 0.25
f32 = jnp.float32
bf16 = jnp.bfloat16
VMEM = pl.BlockSpec(memory_space=pltpu.VMEM)
SMEM = pl.BlockSpec(memory_space=pltpu.SMEM)


def rings(mesh):
    n_tx, n_ty = mesh.shape["tx"], mesh.shape["ty"]
    half = n_ty // 2

    def lin(a, b, m):
        return (a * n_ty + b) * 2 + m

    def perm(move):
        pairs = [
            ((a, b, m), move(a, b, m)) for a in range(n_tx) for b in range(n_ty) for m in range(2)
        ]
        near = [(s, t) for s, t in pairs if abs(s[0] - t[0]) <= 1 and abs(s[1] - t[1]) <= 1]
        return [(lin(*s), lin(*t)) for s, t in near]

    def side(b, d, m):
        other = (b + d) % n_ty
        return other, (1 - m if b // half != other // half else m)

    return {
        "up": perm(lambda a, b, m: ((a - 1) % n_tx, b, m)),
        "down": perm(lambda a, b, m: ((a + 1) % n_tx, b, m)),
        "left": perm(lambda a, b, m: (a, *side(b, -1, m))),
        "right": perm(lambda a, b, m: (a, *side(b, 1, m))),
        "core": perm(lambda a, b, m: (a ^ 1, b, m)),
        "swap": perm(lambda a, b, m: (a, b, 1 - m)),
    }


def split(x):
    high = x.astype(bf16)
    return high, (x - high.astype(f32)).astype(bf16)


def tables():
    half = W // 2
    k, l = np.arange(half)[:, None], np.arange(half)[None, :]
    out = []
    for shift in (0, 1):
        angle = (k * (2 * l + shift) % W) * (2.0 * math.pi / W)
        re, im = np.cos(angle) / math.sqrt(W), -np.sin(angle) / math.sqrt(W)
        block = np.block([[re, im], [-im, re]])
        for mat in (block, block.T):
            high = mat.astype(jnp.bfloat16)
            out += [high, (mat - high.astype(np.float64)).astype(jnp.bfloat16)]
    return out


def dot(a, b):
    return jnp.dot(a, b, preferred_element_type=f32)


def rows_times(x, table):
    xh, xl = split(x)
    high, low = table
    return dot(xh, high) + dot(xh, low) + dot(xl, high)


def cols_times(table, x):
    xh, xl = split(x)
    high, low = table
    return dot(high, xh) + dot(low, xh) + dot(high, xl)


def forward(re, im, even, even_t, odd, odd_t):
    h = W // 2

    def lanes(x, y):
        return jnp.concatenate([x, y], axis=1)

    def stack(x, y):
        return jnp.concatenate([x, y], axis=0)

    e = rows_times(lanes(re[:, :h] + re[:, h:], im[:, :h] + im[:, h:]), even)
    o = rows_times(lanes(re[:, :h] - re[:, h:], im[:, :h] - im[:, h:]), odd)
    re, im = lanes(e[:, :h], o[:, :h]), lanes(e[:, h:], o[:, h:])
    e = cols_times(even_t, stack(re[:h] + re[h:], im[:h] + im[h:]))
    o = cols_times(odd_t, stack(re[:h] - re[h:], im[:h] - im[h:]))
    return stack(e[:h], o[:h]), stack(e[h:], o[h:])


def backward(re, im, even, even_t, odd, odd_t):
    h = W // 2

    def lanes(x, y):
        return jnp.concatenate([x, y], axis=1)

    def stack(x, y):
        return jnp.concatenate([x, y], axis=0)

    a = rows_times(lanes(re[:, :h], im[:, :h]), even_t)
    b = rows_times(lanes(re[:, h:], im[:, h:]), odd_t)
    p, n = a + b, a - b
    re, im = lanes(p[:, :h], n[:, :h]), lanes(p[:, h:], n[:, h:])
    a = cols_times(even, stack(re[:h], im[:h]))
    b = cols_times(odd, stack(re[h:], im[h:]))
    p, n = a + b, a - b
    return stack(p[:h], n[:h]), stack(p[h:], n[h:])


def iota(axis):
    return lax.broadcasted_iota(jnp.int32, (W, W), axis)


def window(obj, c, right, q, s):
    lane = iota(1)
    last = lax.axis_index("ty") == lax.axis_size("ty") - 1
    here = obj[c, :, pl.ds(pl.multiple_of(q * W, W), W)]
    nxt = obj[c, :, pl.ds(pl.multiple_of(jnp.minimum(q + 1, 3) * W, W), W)]
    nxt = jnp.where(q == 3, jnp.where(last, 0.0, right[...]), nxt)
    return jnp.where(lane >= s, here, nxt)


def place(table, slot):
    col0 = table[slot, 1]
    return table[slot, 0], col0 // W, lax.rem(col0, W)


def rim_rows(out, at, obj, c, row, right, left):
    last = lax.axis_index("ty") == lax.axis_size("ty") - 1
    first = lax.axis_index("ty") == 0
    for k in range(4):
        out[at + k : at + k + 1, :] = obj[c, row : row + 1, k * W : (k + 1) * W]
    out[at + 4 : at + 5, :] = jnp.where(last, 0.0, right[row : row + 1, :])
    out[at + 5 : at + 6, :] = jnp.where(first, 0.0, left[c : c + 1, :])
    out[at + 6 : at + 8, :] = jnp.zeros((2, W), f32)


def edge_body(obj, out):
    cols = obj.shape[2]
    for c in range(2):
        out[c : c + 1, :] = obj[c, :, cols - 128 : cols].T[127:128, :]
    out[2:8, :] = jnp.zeros((6, W), f32)


def send_body(c, above, obj, *refs):
    _, q, s = place(above, lax.axis_index("mode"))
    out = refs[c + 1 + c]
    out[0:W, :] = window(obj, c, refs[c], q, s)
    if c == 1:
        for d in range(2):
            rim_rows(out, W + 8 * d, obj, d, 0, refs[d], refs[2])
            rim_rows(refs[4], 8 * d, obj, d, W - 1, refs[d], refs[2])


def main_body(offs, counts, obj, right_0, right_1, below_0, below_1, probe_a, probe_b, probe_c, meas, *refs):
    mats, (grad_0, grad_1, wave) = refs[:8], refs[8:]
    m = lax.axis_index("mode")
    last_tx = lax.axis_index("tx") == lax.axis_size("tx") - 1
    row0, q, s = place(offs, m)
    live = jnp.where(m < counts[0, 0], 1.0, 0.0).astype(f32)
    lane, row = iota(1), iota(0)
    patch = []
    for c, right, below in ((0, right_0, below_0), (1, right_1, below_1)):
        low = jnp.where(last_tx, 0.0, below[0:W, :])
        rolled = jnp.where(row >= row0, window(obj, c, right, q, s), low)
        rolled = pltpu.roll(rolled, lax.rem(W - row0, W), 0)
        patch.append(pltpu.roll(rolled, lax.rem(W - s, W), 1))

    def probe(k, c):
        return (probe_a[0, c], probe_a[1, c], probe_b[0, c], probe_c[0, c])[k]

    tabs = [(mats[2 * k][...], mats[2 * k + 1][...]) for k in range(4)]
    power = jnp.zeros((W, W), f32)
    for k in range(4):
        pr, pi = probe(k, 0), probe(k, 1)
        wr, wi = forward(pr * patch[0] - pi * patch[1], pr * patch[1] + pi * patch[0], *tabs)
        wave[k, 0] = wr
        wave[k, 1] = wi
        power = power + wr * wr + wi * wi
    resid = power - meas[...]
    grad = [jnp.zeros((W, W), f32), jnp.zeros((W, W), f32)]
    for k in range(4):
        pr, pi = probe(k, 0), probe(k, 1)
        br, bi = backward(resid * wave[k, 0], resid * wave[k, 1], *tabs)
        grad[0] = grad[0] + pr * br + pi * bi
        grad[1] = grad[1] + pr * bi - pi * br
    for g, out in ((grad[0], grad_0), (grad[1], grad_1)):
        out[...] = pltpu.roll(pltpu.roll(g * live, row0, 0), s, 1)


def sort_body(meas, out):
    m = lax.axis_index("mode")
    h = W // 2
    lane, row = iota(1), iota(0)

    def nth(k):
        return jnp.where(k < h, 2 * k, 2 * k - W + 1)

    pick_cols = jnp.where(row == nth(lane), 1.0, 0.0).astype(bf16)
    pick_rows = jnp.where(lane == nth(row), 1.0, 0.0).astype(bf16)

    def parts(x):
        for _ in range(3):
            part = x.astype(bf16)
            x = x - part.astype(f32)
            yield part

    x = sum(dot(part, pick_cols) for part in parts(meas[0, 0, m]))
    out[...] = sum(dot(pick_rows, part) for part in parts(x))


def spill_body(n, offs, above, *refs):
    m = lax.axis_index("mode")
    tx = lax.axis_index("tx")
    lane, row = iota(1), iota(0)
    total = jnp.zeros((W, W), f32)
    for k, slot in enumerate((m, 1 - m)[:n]):
        row0, q, s = place(offs, slot)
        total = total + jnp.where((q == 3) & (lane < s) & (row >= row0), refs[k][...], 0.0)
        row0, q, s = place(above, slot)
        keep = (q == 3) & (lane < s) & (row < row0) & (tx > 0)
        total = total + jnp.where(keep, refs[n + k][...], 0.0)
    refs[2 * n][...] = total


def take(out, ref, spot, rows):
    _, q, s = spot
    lane = iota(1)
    value = ref[...]
    here = pl.ds(pl.multiple_of(q * W, W), W)
    out[:, here] = out[:, here] - step_size * jnp.where(rows & (lane >= s), value, 0.0)
    nxt = pl.ds(pl.multiple_of(jnp.minimum(q + 1, 3) * W, W), W)
    keep = rows & (lane < s) & (q < 3)
    out[:, nxt] = out[:, nxt] - step_size * jnp.where(keep, value, 0.0)


def prior_body(c, filt, offs, obj, right, left, up, down, own, out):
    tx, ty = lax.axis_index("tx"), lax.axis_index("ty")
    n_tx, n_ty = lax.axis_size("tx"), lax.axis_size("ty")
    cols = obj.shape[2]
    shape = (W, cols)
    lane = lax.broadcasted_iota(jnp.int32, shape, 1)
    row = lax.broadcasted_iota(jnp.int32, shape, 0)
    taps = [[filt[i, k] for i in range(4)] for k in range(filt.shape[1])]
    g = [[sum(tap[i] * tap[j] for tap in taps) for j in range(4)] for i in range(4)]

    def beside(x, before, after):
        one_left = jnp.where(lane == 0, before, pltpu.roll(x, 1, 1))
        one_right = jnp.where(lane == cols - 1, after, pltpu.roll(x, cols - 1, 1))
        return one_left, one_right

    spot = place(offs, lax.axis_index("mode"))
    x = obj[c]
    after = jnp.where(ty == n_ty - 1, 0.0, right[:, 0:1])
    edge = jnp.broadcast_to(left[c : c + 1, :], (128, W)).T
    before = jnp.where(ty == 0, 0.0, edge[:, 0:1])

    def line(rim, flag, at):
        rim = jnp.where(flag, 0.0, rim)
        whole = jnp.concatenate([rim[k : k + 1, :] for k in range(4)], axis=1)
        return whole, rim[5:6, at : at + 1], rim[4:5, 0:1]

    u_mid, u_left, u_right = line(up[8 * c : 8 * c + 8, :], tx == 0, W - 1)
    d_mid, d_left, d_right = line(down[W + 8 * c : W + 8 * c + 8, :], tx == n_tx - 1, 0)
    xl, xr = beside(x, before, after)

    def over(mid, edge):
        return jnp.where(row == 0, edge, pltpu.roll(mid, 1, 0))

    def under(mid, edge):
        return jnp.where(row == W - 1, edge, pltpu.roll(mid, W - 1, 0))

    def shift_line(mid, b, a):
        l1 = lax.broadcasted_iota(jnp.int32, (1, cols), 1)
        return (
            jnp.where(l1 == 0, b, pltpu.roll(mid, 1, 1)),
            jnp.where(l1 == cols - 1, a, pltpu.roll(mid, cols - 1, 1)),
        )

    ul, ur = shift_line(u_mid, u_left, u_right)
    dl, dr = shift_line(d_mid, d_left, d_right)
    xu, xd = over(x, u_mid), under(x, d_mid)
    xul, xur = over(xl, ul), over(xr, ur)
    xdl, xdr = under(xl, dl), under(xr, dr)
    in_col = (lane > 0) | (ty > 0)
    in_row = (row > 0) | (tx > 0)
    total = g[0][0] * x + g[0][1] * xr + g[0][2] * xd + g[0][3] * xdr
    total += jnp.where(in_col, g[1][0] * xl + g[1][1] * x + g[1][2] * xdl + g[1][3] * xd, 0.0)
    total += jnp.where(in_row, g[2][0] * xu + g[2][1] * xur + g[2][2] * x + g[2][3] * xr, 0.0)
    total += jnp.where(
        in_row & in_col, g[3][0] * xul + g[3][1] * xu + g[3][2] * xl + g[3][3] * x, 0.0
    )
    out[...] = x - step_size * total
    take(out, own, spot, iota(0) >= spot[0])


def fold_body(offs, above, base, own_p, up_m, up_p, out):
    m = lax.axis_index("mode")
    row = iota(0)
    mine = place(offs, 1 - m)
    out[...] = base[...]
    take(out, own_p, mine, row >= mine[0])
    for ref, slot in ((up_m, m), (up_p, 1 - m)):
        over = place(above, slot)
        take(out, ref, over, (row < over[0]) & (lax.axis_index("tx") > 0))


def mid_body(offs, above, base, own_p, up_m, up_p, left_0, done, out, first):
    part = out.at[0]
    fold_body(offs, above, base, own_p, up_m, up_p, part)
    first[0] = part[:, 0:W] - step_size * jnp.where(lax.axis_index("ty") > 0, left_0[...], 0.0)
    out[1] = done[...]
    first[1] = done[:, 0:W]


def final_body(mid, first, left_0, left_1, out, buf, sems):
    ty = lax.axis_index("ty")
    stores = [pltpu.make_async_copy(buf.at[c], out.at[c, :, 0:W], sems.at[c]) for c in range(2)]
    for c, left in enumerate((left_0, left_1)):
        buf[c] = first[c] - step_size * jnp.where(ty > 0, left[...], 0.0)
        stores[c].start()
    for store in stores:
        store.wait()


def call(body, shapes, in_specs, limit, flops, bytes_accessed, scratch=(), out_spec=VMEM, aliases={}):
    many = isinstance(shapes, list)
    outs = [jax.ShapeDtypeStruct(s, f32) for s in (shapes if many else [shapes])]
    return pl.pallas_call(
        body,
        out_shape=outs if many else outs[0],
        in_specs=in_specs,
        out_specs=[out_spec] * len(outs) if many else out_spec,
        scratch_shapes=list(scratch),
        input_output_aliases=aliases,
        compiler_params=pltpu.CompilerParams(vmem_limit_bytes=limit << 20),
        cost_estimate=pl.CostEstimate(flops=flops, bytes_accessed=bytes_accessed, transcendentals=0),
    )


def local(ring, obj, probe, intensity, offsets, counts, filters):
    def go(value, where):
        return lax.ppermute(value, axes, ring[where])

    tabs = [jnp.asarray(t) for t in tables()]

    rows, cols = obj.shape[1:]
    piece = (W, W)
    whole = (2, rows, cols)
    offs = offsets.reshape(2, 2)
    right = [go(obj[0, :, :W], "left")]
    right.append(go(lax.optimization_barrier(obj)[1, :, :W], "left"))
    core = lax.rem(lax.axis_index("tx"), 2)
    probe_b = go(lax.dynamic_slice_in_dim(probe, core, 1, 0), "swap")
    probe_c = go(probe_b, "core")
    above = go(offs, "down")
    edge = call(edge_body, (8, W), [VMEM], 8, 1 << 16, 1 << 18)(obj)
    left = go(edge, "right")
    filt = filters.T
    meas = call(sort_body, piece, [VMEM], 8, 1 << 26, 3 << 18)(intensity)
    up_0 = call(
        functools.partial(send_body, 0), piece, [SMEM] + [VMEM] * 2, 8, 1 << 20, 2 << 20
    )(above, obj, right[0])
    below_0 = go(up_0, "up")
    up_1, rim = call(
        functools.partial(send_body, 1),
        [(W + 16, W), (16, W)],
        [SMEM] + [VMEM] * 4,
        8,
        1 << 20,
        2 << 20,
    )(above, obj, *right, left)
    below_1 = go(up_1, "up")
    over = go(rim, "down")
    g0, g1 = call(
        main_body,
        [piece] * 2,
        [SMEM, SMEM] + [VMEM] * 17,
        16,
        5 << 30,
        12 << 20,
        [pltpu.VMEM((4, 2, W, W), f32)],
    )(offs, counts, obj, *right, below_0, below_1, probe, probe_b, probe_c, meas, *tabs)
    p1, b0 = go(g1, "swap"), go(g0, "down")
    p0, b1 = go(g0, "swap"), go(g1, "down")
    base = [
        call(
            functools.partial(prior_body, c), (rows, cols), [SMEM] * 2 + [VMEM] * 6, 12, 1 << 27, 8 << 20
        )(filt, offs, obj, right[c], left, over, below_1, g)
        for c, g in ((0, g0), (1, g1))
    ]
    c1, c0 = go(p1, "down"), go(p0, "down")

    def spill(n, *args):
        specs = [SMEM, SMEM] + [VMEM] * (2 * n)
        kernel = call(functools.partial(spill_body, n), piece, specs, 8, 1 << 18, 1 << 20)
        return kernel(offs, above, *args)

    left_m0 = go(spill(1, g0, b0), "right")
    left_p0 = go(left_m0, "swap")
    left_1 = go(spill(2, g1, p1, b1, c1), "right")
    any_space = pl.BlockSpec(memory_space=pl.ANY)
    fold = call(fold_body, (rows, cols), [SMEM, SMEM] + [VMEM] * 4, 8, 1 << 20, 4 << 20)(
        offs, above, base[1], p1, b1, c1
    )
    mid, first = call(
        mid_body, [whole, (2, W, W)], [SMEM, SMEM] + [VMEM] * 6, 12, 1 << 24, 10 << 20
    )(offs, above, base[0], p0, b0, c0, left_m0, fold)
    return call(
        final_body,
        whole,
        [any_space] + [VMEM] * 3,
        8,
        1 << 18,
        2 << 20,
        [pltpu.VMEM((2, W, W), f32), pltpu.SemaphoreType.DMA((2,))],
        any_space,
        {0: 0},
    )(mid, first, left_p0, left_1)


def solution(mesh):
    placed = (
        P(None, "tx", "ty"),
        P("mode", None, None, None),
        P("tx", "ty", None, None, None),
        P("tx", "ty", None, None),
        P("tx", "ty"),
        P(),
    )

    def body(*args):
        return local(rings(mesh), *args)

    return jax.shard_map(
        body, mesh=mesh, in_specs=placed, out_specs=P(None, "tx", "ty"), check_vma=False
    )
```

```python
import functools
import math

import jax
import jax.numpy as jnp
import numpy as np
from jax import lax
from jax.experimental import pallas as pl
from jax.experimental.pallas import tpu as pltpu
from jax.sharding import PartitionSpec as P


W = 256
axes = ("tx", "ty", "mode")
step_size = 0.25
f32 = jnp.float32
bf16 = jnp.bfloat16
VMEM = pl.BlockSpec(memory_space=pltpu.VMEM)
SMEM = pl.BlockSpec(memory_space=pltpu.SMEM)


def rings(mesh):
    n_tx, n_ty = mesh.shape["tx"], mesh.shape["ty"]
    half = n_ty // 2

    def lin(a, b, m):
        return (a * n_ty + b) * 2 + m

    def perm(move):
        return [
            (lin(a, b, m), lin(*move(a, b, m)))
            for a in range(n_tx)
            for b in range(n_ty)
            for m in range(2)
        ]

    def side(b, d, m):
        other = (b + d) % n_ty
        return other, (1 - m if b // half != other // half else m)

    return {
        "up": perm(lambda a, b, m: ((a - 1) % n_tx, b, m)),
        "down": perm(lambda a, b, m: ((a + 1) % n_tx, b, m)),
        "left": perm(lambda a, b, m: (a, *side(b, -1, m))),
        "right": perm(lambda a, b, m: (a, *side(b, 1, m))),
        "core": perm(lambda a, b, m: (a ^ 1, b, m)),
        "swap": perm(lambda a, b, m: (a, b, 1 - m)),
    }


def split(x):
    high = x.astype(bf16)
    return high, (x - high.astype(f32)).astype(bf16)


def tables():
    half = W // 2
    k, l = np.arange(half)[:, None], np.arange(half)[None, :]
    out = []
    for shift in (0, 1):
        angle = (k * (2 * l + shift) % W) * (2.0 * math.pi / W)
        re, im = np.cos(angle) / math.sqrt(W), -np.sin(angle) / math.sqrt(W)
        block = np.block([[re, im], [-im, re]])
        for mat in (block, block.T):
            high = mat.astype(jnp.bfloat16)
            out += [high, (mat - high.astype(np.float64)).astype(jnp.bfloat16)]
    return out


def dot(a, b):
    return jnp.dot(a, b, preferred_element_type=f32)


def rows_times(x, table):
    xh, xl = split(x)
    high, low = table
    return dot(xh, high) + dot(xh, low) + dot(xl, high)


def cols_times(table, x):
    xh, xl = split(x)
    high, low = table
    return dot(high, xh) + dot(low, xh) + dot(high, xl)


def forward(re, im, even, even_t, odd, odd_t):
    h = W // 2

    def lanes(x, y):
        return jnp.concatenate([x, y], axis=1)

    def stack(x, y):
        return jnp.concatenate([x, y], axis=0)

    e = rows_times(lanes(re[:, :h] + re[:, h:], im[:, :h] + im[:, h:]), even)
    o = rows_times(lanes(re[:, :h] - re[:, h:], im[:, :h] - im[:, h:]), odd)
    re, im = lanes(e[:, :h], o[:, :h]), lanes(e[:, h:], o[:, h:])
    e = cols_times(even_t, stack(re[:h] + re[h:], im[:h] + im[h:]))
    o = cols_times(odd_t, stack(re[:h] - re[h:], im[:h] - im[h:]))
    return stack(e[:h], o[:h]), stack(e[h:], o[h:])


def backward(re, im, even, even_t, odd, odd_t):
    h = W // 2

    def lanes(x, y):
        return jnp.concatenate([x, y], axis=1)

    def stack(x, y):
        return jnp.concatenate([x, y], axis=0)

    a = rows_times(lanes(re[:, :h], im[:, :h]), even_t)
    b = rows_times(lanes(re[:, h:], im[:, h:]), odd_t)
    p, n = a + b, a - b
    re, im = lanes(p[:, :h], n[:, :h]), lanes(p[:, h:], n[:, h:])
    a = cols_times(even, stack(re[:h], im[:h]))
    b = cols_times(odd, stack(re[h:], im[h:]))
    p, n = a + b, a - b
    return stack(p[:h], n[:h]), stack(p[h:], n[h:])


def iota(axis):
    return lax.broadcasted_iota(jnp.int32, (W, W), axis)


def window(obj, c, right, q, s):
    lane = iota(1)
    last = lax.axis_index("ty") == lax.axis_size("ty") - 1
    here = obj[c, :, pl.ds(pl.multiple_of(q * W, W), W)]
    nxt = obj[c, :, pl.ds(pl.multiple_of(jnp.minimum(q + 1, 3) * W, W), W)]
    nxt = jnp.where(q == 3, jnp.where(last, 0.0, right[...]), nxt)
    return jnp.where(lane >= s, here, nxt)


def place(table, slot):
    col0 = table[slot, 1]
    return table[slot, 0], col0 // W, lax.rem(col0, W)


def rim_rows(out, at, obj, c, row, right, left):
    last = lax.axis_index("ty") == lax.axis_size("ty") - 1
    first = lax.axis_index("ty") == 0
    for k in range(4):
        out[at + k : at + k + 1, :] = obj[c, row : row + 1, k * W : (k + 1) * W]
    out[at + 4 : at + 5, :] = jnp.where(last, 0.0, right[row : row + 1, :])
    out[at + 5 : at + 6, :] = jnp.where(first, 0.0, left[c : c + 1, :])
    out[at + 6 : at + 8, :] = jnp.zeros((2, W), f32)


def edge_body(obj, out):
    cols = obj.shape[2]
    for c in range(2):
        out[c : c + 1, :] = obj[c, :, cols - 128 : cols].T[127:128, :]
    out[2:8, :] = jnp.zeros((6, W), f32)


def send_body(c, above, obj, *refs):
    _, q, s = place(above, lax.axis_index("mode"))
    out = refs[c + 1 + c]
    out[0:W, :] = window(obj, c, refs[c], q, s)
    if c == 1:
        for d in range(2):
            rim_rows(out, W + 8 * d, obj, d, 0, refs[d], refs[2])
            rim_rows(refs[4], 8 * d, obj, d, W - 1, refs[d], refs[2])


def main_body(offs, counts, obj, right_0, right_1, below_0, below_1, probe_a, probe_b, probe_c, meas, *refs):
    mats, (grad_0, grad_1, wave) = refs[:8], refs[8:]
    m = lax.axis_index("mode")
    last_tx = lax.axis_index("tx") == lax.axis_size("tx") - 1
    row0, q, s = place(offs, m)
    live = jnp.where(m < counts[0, 0], 1.0, 0.0).astype(f32)
    lane, row = iota(1), iota(0)
    patch = []
    for c, right, below in ((0, right_0, below_0), (1, right_1, below_1)):
        low = jnp.where(last_tx, 0.0, below[0:W, :])
        rolled = jnp.where(row >= row0, window(obj, c, right, q, s), low)
        rolled = pltpu.roll(rolled, lax.rem(W - row0, W), 0)
        patch.append(pltpu.roll(rolled, lax.rem(W - s, W), 1))

    def probe(k, c):
        return (probe_a[0, c], probe_a[1, c], probe_b[0, c], probe_c[0, c])[k]

    tabs = [(mats[2 * k][...], mats[2 * k + 1][...]) for k in range(4)]
    power = jnp.zeros((W, W), f32)
    for k in range(4):
        pr, pi = probe(k, 0), probe(k, 1)
        wr, wi = forward(pr * patch[0] - pi * patch[1], pr * patch[1] + pi * patch[0], *tabs)
        wave[k, 0] = wr
        wave[k, 1] = wi
        power = power + wr * wr + wi * wi
    resid = power - meas[...]
    grad = [jnp.zeros((W, W), f32), jnp.zeros((W, W), f32)]
    for k in range(4):
        pr, pi = probe(k, 0), probe(k, 1)
        br, bi = backward(resid * wave[k, 0], resid * wave[k, 1], *tabs)
        grad[0] = grad[0] + pr * br + pi * bi
        grad[1] = grad[1] + pr * bi - pi * br
    for g, out in ((grad[0], grad_0), (grad[1], grad_1)):
        out[...] = pltpu.roll(pltpu.roll(g * live, row0, 0), s, 1)


def sort_body(meas, out):
    m = lax.axis_index("mode")
    h = W // 2
    lane, row = iota(1), iota(0)

    def nth(k):
        return jnp.where(k < h, 2 * k, 2 * k - W + 1)

    pick_cols = jnp.where(row == nth(lane), 1.0, 0.0).astype(bf16)
    pick_rows = jnp.where(lane == nth(row), 1.0, 0.0).astype(bf16)

    def parts(x):
        for _ in range(3):
            part = x.astype(bf16)
            x = x - part.astype(f32)
            yield part

    x = sum(dot(part, pick_cols) for part in parts(meas[0, 0, m]))
    out[...] = sum(dot(pick_rows, part) for part in parts(x))


def spill_body(n, offs, above, *refs):
    m = lax.axis_index("mode")
    tx = lax.axis_index("tx")
    lane, row = iota(1), iota(0)
    total = jnp.zeros((W, W), f32)
    for k, slot in enumerate((m, 1 - m)[:n]):
        row0, q, s = place(offs, slot)
        total = total + jnp.where((q == 3) & (lane < s) & (row >= row0), refs[k][...], 0.0)
        row0, q, s = place(above, slot)
        keep = (q == 3) & (lane < s) & (row < row0) & (tx > 0)
        total = total + jnp.where(keep, refs[n + k][...], 0.0)
    refs[2 * n][...] = total


def take(out, ref, spot, rows):
    _, q, s = spot
    lane = iota(1)
    value = ref[...]
    here = pl.ds(pl.multiple_of(q * W, W), W)
    out[:, here] = out[:, here] - step_size * jnp.where(rows & (lane >= s), value, 0.0)
    nxt = pl.ds(pl.multiple_of(jnp.minimum(q + 1, 3) * W, W), W)
    keep = rows & (lane < s) & (q < 3)
    out[:, nxt] = out[:, nxt] - step_size * jnp.where(keep, value, 0.0)


def prior_body(c, filt, offs, obj, right, left, up, down, own, out):
    tx, ty = lax.axis_index("tx"), lax.axis_index("ty")
    n_tx, n_ty = lax.axis_size("tx"), lax.axis_size("ty")
    cols = obj.shape[2]
    shape = (W, cols)
    lane = lax.broadcasted_iota(jnp.int32, shape, 1)
    row = lax.broadcasted_iota(jnp.int32, shape, 0)
    taps = [[filt[i, k] for i in range(4)] for k in range(filt.shape[1])]
    g = [[sum(tap[i] * tap[j] for tap in taps) for j in range(4)] for i in range(4)]

    def beside(x, before, after):
        one_left = jnp.where(lane == 0, before, pltpu.roll(x, 1, 1))
        one_right = jnp.where(lane == cols - 1, after, pltpu.roll(x, cols - 1, 1))
        return one_left, one_right

    spot = place(offs, lax.axis_index("mode"))
    x = obj[c]
    after = jnp.where(ty == n_ty - 1, 0.0, right[:, 0:1])
    edge = jnp.broadcast_to(left[c : c + 1, :], (128, W)).T
    before = jnp.where(ty == 0, 0.0, edge[:, 0:1])

    def line(rim, flag, at):
        rim = jnp.where(flag, 0.0, rim)
        whole = jnp.concatenate([rim[k : k + 1, :] for k in range(4)], axis=1)
        return whole, rim[5:6, at : at + 1], rim[4:5, 0:1]

    u_mid, u_left, u_right = line(up[8 * c : 8 * c + 8, :], tx == 0, W - 1)
    d_mid, d_left, d_right = line(down[W + 8 * c : W + 8 * c + 8, :], tx == n_tx - 1, 0)
    xl, xr = beside(x, before, after)

    def over(mid, edge):
        return jnp.where(row == 0, edge, pltpu.roll(mid, 1, 0))

    def under(mid, edge):
        return jnp.where(row == W - 1, edge, pltpu.roll(mid, W - 1, 0))

    def shift_line(mid, b, a):
        l1 = lax.broadcasted_iota(jnp.int32, (1, cols), 1)
        return (
            jnp.where(l1 == 0, b, pltpu.roll(mid, 1, 1)),
            jnp.where(l1 == cols - 1, a, pltpu.roll(mid, cols - 1, 1)),
        )

    ul, ur = shift_line(u_mid, u_left, u_right)
    dl, dr = shift_line(d_mid, d_left, d_right)
    xu, xd = over(x, u_mid), under(x, d_mid)
    xul, xur = over(xl, ul), over(xr, ur)
    xdl, xdr = under(xl, dl), under(xr, dr)
    in_col = (lane > 0) | (ty > 0)
    in_row = (row > 0) | (tx > 0)
    total = g[0][0] * x + g[0][1] * xr + g[0][2] * xd + g[0][3] * xdr
    total += jnp.where(in_col, g[1][0] * xl + g[1][1] * x + g[1][2] * xdl + g[1][3] * xd, 0.0)
    total += jnp.where(in_row, g[2][0] * xu + g[2][1] * xur + g[2][2] * x + g[2][3] * xr, 0.0)
    total += jnp.where(
        in_row & in_col, g[3][0] * xul + g[3][1] * xu + g[3][2] * xl + g[3][3] * x, 0.0
    )
    out[...] = x - step_size * total
    take(out, own, spot, iota(0) >= spot[0])


def fold(c, offs, above, base, own_p, up_m, up_p, out, first, buf, sem):
    m = lax.axis_index("mode")
    tx = lax.axis_index("tx")
    row = iota(0)
    mine = place(offs, 1 - m)
    buf[...] = base[...]
    take(buf, own_p, mine, row >= mine[0])
    for ref, slot in ((up_m, m), (up_p, 1 - m)):
        over = place(above, slot)
        take(buf, ref, over, (row < over[0]) & (tx > 0))
    store = pltpu.make_async_copy(buf.at[:, W:], out.at[c, :, W:], sem)
    store.start()
    first[...] = buf[:, 0:W]
    store.wait()


def fold_body(*refs):
    fold(1, *refs)


def mid_body(whole, left_0, *refs):
    fold(0, *refs)
    first = refs[-3]
    first[...] = first[...] - step_size * jnp.where(lax.axis_index("ty") > 0, left_0[...], 0.0)


def final_body(mid, first_0, first_1, left_0, left_1, out, buf, sems):
    ty = lax.axis_index("ty")
    stores = [pltpu.make_async_copy(buf.at[c], out.at[c, :, 0:W], sems.at[c]) for c in range(2)]
    for c, (first, left) in enumerate(((first_0, left_0), (first_1, left_1))):
        buf[c] = first[...] - step_size * jnp.where(ty > 0, left[...], 0.0)
        stores[c].start()
    for store in stores:
        store.wait()


def call(body, shapes, in_specs, limit, flops, bytes_accessed, scratch=(), out_spec=VMEM, aliases={}):
    many = isinstance(shapes, list)
    outs = [jax.ShapeDtypeStruct(s, f32) for s in (shapes if many else [shapes])]
    return pl.pallas_call(
        body,
        out_shape=outs if many else outs[0],
        in_specs=in_specs,
        out_specs=out_spec if isinstance(out_spec, list) else ([out_spec] * len(outs) if many else out_spec),
        scratch_shapes=list(scratch),
        input_output_aliases=aliases,
        compiler_params=pltpu.CompilerParams(vmem_limit_bytes=limit << 20),
        cost_estimate=pl.CostEstimate(flops=flops, bytes_accessed=bytes_accessed, transcendentals=0),
    )


def local(ring, obj, probe, intensity, offsets, counts, filters):
    def go(value, where):
        return lax.ppermute(value, axes, ring[where])

    tabs = [jnp.asarray(t) for t in tables()]

    rows, cols = obj.shape[1:]
    piece = (W, W)
    whole = (2, rows, cols)
    offs = offsets.reshape(2, 2)
    right = [go(obj[0, :, :W], "left")]
    right.append(go(lax.optimization_barrier(obj)[1, :, :W], "left"))
    core = lax.rem(lax.axis_index("tx"), 2)
    probe_b = go(lax.dynamic_slice_in_dim(probe, core, 1, 0), "swap")
    probe_c = go(probe_b, "core")
    above = go(offs, "down")
    edge = call(edge_body, (8, W), [VMEM], 8, 1 << 16, 1 << 18)(obj)
    left = go(edge, "right")
    filt = filters.T
    meas = call(sort_body, piece, [VMEM], 8, 1 << 26, 3 << 18)(intensity)
    up_0 = call(
        functools.partial(send_body, 0), piece, [SMEM] + [VMEM] * 2, 8, 1 << 20, 2 << 20
    )(above, obj, right[0])
    below_0 = go(up_0, "up")
    up_1, rim = call(
        functools.partial(send_body, 1),
        [(W + 16, W), (16, W)],
        [SMEM] + [VMEM] * 4,
        8,
        1 << 20,
        2 << 20,
    )(above, obj, *right, left)
    below_1 = go(up_1, "up")
    over = go(rim, "down")
    g0, g1 = call(
        main_body,
        [piece] * 2,
        [SMEM, SMEM] + [VMEM] * 17,
        16,
        5 << 30,
        12 << 20,
        [pltpu.VMEM((4, 2, W, W), f32)],
    )(offs, counts, obj, *right, below_0, below_1, probe, probe_b, probe_c, meas, *tabs)
    p1, b0 = go(g1, "swap"), go(g0, "down")
    p0, b1 = go(g0, "swap"), go(g1, "down")
    base = [
        call(
            functools.partial(prior_body, c), (rows, cols), [SMEM] * 2 + [VMEM] * 6, 12, 1 << 27, 8 << 20
        )(filt, offs, obj, right[c], left, over, below_1, g)
        for c, g in ((0, g0), (1, g1))
    ]
    c1, c0 = go(p1, "down"), go(p0, "down")

    def spill(n, *args):
        specs = [SMEM, SMEM] + [VMEM] * (2 * n)
        kernel = call(functools.partial(spill_body, n), piece, specs, 8, 1 << 18, 1 << 20)
        return kernel(offs, above, *args)

    left_m0 = go(spill(1, g0, b0), "right")
    left_p0 = go(left_m0, "swap")
    left_1 = go(spill(2, g1, p1, b1, c1), "right")
    any_space = pl.BlockSpec(memory_space=pl.ANY)
    store = [pltpu.VMEM((rows, cols), f32), pltpu.SemaphoreType.DMA]
    spaces = [any_space, VMEM]
    fold, first_1 = call(
        fold_body, [whole, piece], [SMEM, SMEM] + [VMEM] * 4, 8, 1 << 20, 4 << 20, store, spaces
    )(offs, above, base[1], p1, b1, c1)
    mid, first_0 = call(
        mid_body,
        [whole, piece],
        [any_space, VMEM, SMEM, SMEM] + [VMEM] * 4,
        8,
        1 << 24,
        5 << 20,
        store,
        spaces,
        {0: 0},
    )(fold, left_m0, offs, above, base[0], p0, b0, c0)
    return call(
        final_body,
        whole,
        [any_space] + [VMEM] * 4,
        8,
        1 << 18,
        2 << 20,
        [pltpu.VMEM((2, W, W), f32), pltpu.SemaphoreType.DMA((2,))],
        any_space,
        {0: 0},
    )(mid, first_0, first_1, left_p0, left_1)


def solution(mesh):
    placed = (
        P(None, "tx", "ty"),
        P("mode", None, None, None),
        P("tx", "ty", None, None, None),
        P("tx", "ty", None, None),
        P("tx", "ty"),
        P(),
    )

    def body(*args):
        return local(rings(mesh), *args)

    return jax.shard_map(
        body, mesh=mesh, in_specs=placed, out_specs=P(None, "tx", "ty"), check_vma=False
    )
```

```python
import functools
import math

import jax
import jax.numpy as jnp
import numpy as np
from jax import lax
from jax.experimental import pallas as pl
from jax.experimental.pallas import tpu as pltpu
from jax.sharding import PartitionSpec as P


W = 256
axes = ("tx", "ty", "mode")
step_size = 0.25
f32 = jnp.float32
bf16 = jnp.bfloat16
VMEM = pl.BlockSpec(memory_space=pltpu.VMEM)
SMEM = pl.BlockSpec(memory_space=pltpu.SMEM)


def rings(mesh):
    n_tx, n_ty = mesh.shape["tx"], mesh.shape["ty"]
    half = n_ty // 2

    def lin(a, b, m):
        return (a * n_ty + b) * 2 + m

    def perm(move):
        return [
            (lin(a, b, m), lin(*move(a, b, m)))
            for a in range(n_tx)
            for b in range(n_ty)
            for m in range(2)
        ]

    def side(b, d, m):
        other = (b + d) % n_ty
        return other, (1 - m if b // half != other // half else m)

    return {
        "up": perm(lambda a, b, m: ((a - 1) % n_tx, b, m)),
        "down": perm(lambda a, b, m: ((a + 1) % n_tx, b, m)),
        "left": perm(lambda a, b, m: (a, *side(b, -1, m))),
        "right": perm(lambda a, b, m: (a, *side(b, 1, m))),
        "core": perm(lambda a, b, m: (a ^ 1, b, m)),
        "swap": perm(lambda a, b, m: (a, b, 1 - m)),
    }


def split(x):
    high = x.astype(bf16)
    return high, (x - high.astype(f32)).astype(bf16)


def tables():
    half = W // 2
    k, l = np.arange(half)[:, None], np.arange(half)[None, :]
    out = []
    for shift in (0, 1):
        angle = (k * (2 * l + shift) % W) * (2.0 * math.pi / W)
        re, im = np.cos(angle) / math.sqrt(W), -np.sin(angle) / math.sqrt(W)
        block = np.block([[re, im], [-im, re]])
        for mat in (block, block.T):
            high = mat.astype(jnp.bfloat16)
            out += [high, (mat - high.astype(np.float64)).astype(jnp.bfloat16)]
    return out


def dot(a, b):
    return jnp.dot(a, b, preferred_element_type=f32)


def rows_times(x, table):
    xh, xl = split(x)
    high, low = table
    return dot(xh, high) + dot(xh, low) + dot(xl, high)


def cols_times(table, x):
    xh, xl = split(x)
    high, low = table
    return dot(high, xh) + dot(low, xh) + dot(high, xl)


def forward(re, im, even, even_t, odd, odd_t):
    h = W // 2

    def lanes(x, y):
        return jnp.concatenate([x, y], axis=1)

    def stack(x, y):
        return jnp.concatenate([x, y], axis=0)

    e = rows_times(lanes(re[:, :h] + re[:, h:], im[:, :h] + im[:, h:]), even)
    o = rows_times(lanes(re[:, :h] - re[:, h:], im[:, :h] - im[:, h:]), odd)
    re, im = lanes(e[:, :h], o[:, :h]), lanes(e[:, h:], o[:, h:])
    e = cols_times(even_t, stack(re[:h] + re[h:], im[:h] + im[h:]))
    o = cols_times(odd_t, stack(re[:h] - re[h:], im[:h] - im[h:]))
    return stack(e[:h], o[:h]), stack(e[h:], o[h:])


def backward(re, im, even, even_t, odd, odd_t):
    h = W // 2

    def lanes(x, y):
        return jnp.concatenate([x, y], axis=1)

    def stack(x, y):
        return jnp.concatenate([x, y], axis=0)

    a = rows_times(lanes(re[:, :h], im[:, :h]), even_t)
    b = rows_times(lanes(re[:, h:], im[:, h:]), odd_t)
    p, n = a + b, a - b
    re, im = lanes(p[:, :h], n[:, :h]), lanes(p[:, h:], n[:, h:])
    a = cols_times(even, stack(re[:h], im[:h]))
    b = cols_times(odd, stack(re[h:], im[h:]))
    p, n = a + b, a - b
    return stack(p[:h], n[:h]), stack(p[h:], n[h:])


def iota(axis):
    return lax.broadcasted_iota(jnp.int32, (W, W), axis)


def window(obj, c, right, q, s):
    lane = iota(1)
    last = lax.axis_index("ty") == lax.axis_size("ty") - 1
    here = obj[c, :, pl.ds(pl.multiple_of(q * W, W), W)]
    nxt = obj[c, :, pl.ds(pl.multiple_of(jnp.minimum(q + 1, 3) * W, W), W)]
    nxt = jnp.where(q == 3, jnp.where(last, 0.0, right[...]), nxt)
    return jnp.where(lane >= s, here, nxt)


def place(table, slot):
    col0 = table[slot, 1]
    return table[slot, 0], col0 // W, lax.rem(col0, W)


def rim_rows(out, at, obj, c, row, right, left):
    last = lax.axis_index("ty") == lax.axis_size("ty") - 1
    first = lax.axis_index("ty") == 0
    for k in range(4):
        out[at + k : at + k + 1, :] = obj[c, row : row + 1, k * W : (k + 1) * W]
    out[at + 4 : at + 5, :] = jnp.where(last, 0.0, right[row : row + 1, :])
    out[at + 5 : at + 6, :] = jnp.where(first, 0.0, left[c : c + 1, :])
    out[at + 6 : at + 8, :] = jnp.zeros((2, W), f32)


def edge_body(obj, out):
    cols = obj.shape[2]
    for c in range(2):
        out[c : c + 1, :] = obj[c, :, cols - 128 : cols].T[127:128, :]
    out[2:8, :] = jnp.zeros((6, W), f32)


def send_body(c, above, obj, *refs):
    _, q, s = place(above, lax.axis_index("mode"))
    out = refs[c + 1 + c]
    out[0:W, :] = window(obj, c, refs[c], q, s)
    if c == 1:
        for d in range(2):
            rim_rows(out, W + 8 * d, obj, d, 0, refs[d], refs[2])
            rim_rows(refs[4], 8 * d, obj, d, W - 1, refs[d], refs[2])


def main_body(offs, counts, obj, right_0, right_1, below_0, below_1, probe_a, probe_b, probe_c, meas, *refs):
    mats, (grad_0, grad_1, wave) = refs[:8], refs[8:]
    m = lax.axis_index("mode")
    last_tx = lax.axis_index("tx") == lax.axis_size("tx") - 1
    row0, q, s = place(offs, m)
    live = jnp.where(m < counts[0, 0], 1.0, 0.0).astype(f32)
    lane, row = iota(1), iota(0)
    patch = []
    for c, right, below in ((0, right_0, below_0), (1, right_1, below_1)):
        low = jnp.where(last_tx, 0.0, below[0:W, :])
        rolled = jnp.where(row >= row0, window(obj, c, right, q, s), low)
        rolled = pltpu.roll(rolled, lax.rem(W - row0, W), 0)
        patch.append(pltpu.roll(rolled, lax.rem(W - s, W), 1))

    def probe(k, c):
        return (probe_a[0, c], probe_a[1, c], probe_b[0, c], probe_c[0, c])[k]

    tabs = [(mats[2 * k][...], mats[2 * k + 1][...]) for k in range(4)]
    power = jnp.zeros((W, W), f32)
    for k in range(4):
        pr, pi = probe(k, 0), probe(k, 1)
        wr, wi = forward(pr * patch[0] - pi * patch[1], pr * patch[1] + pi * patch[0], *tabs)
        wave[k, 0] = wr
        wave[k, 1] = wi
        power = power + wr * wr + wi * wi
    resid = power - meas[...]
    grad = [jnp.zeros((W, W), f32), jnp.zeros((W, W), f32)]
    for k in range(4):
        pr, pi = probe(k, 0), probe(k, 1)
        br, bi = backward(resid * wave[k, 0], resid * wave[k, 1], *tabs)
        grad[0] = grad[0] + pr * br + pi * bi
        grad[1] = grad[1] + pr * bi - pi * br
    for g, out in ((grad[0], grad_0), (grad[1], grad_1)):
        out[...] = pltpu.roll(pltpu.roll(g * live, row0, 0), s, 1)


def sort_body(meas, out):
    m = lax.axis_index("mode")
    h = W // 2
    lane, row = iota(1), iota(0)

    def nth(k):
        return jnp.where(k < h, 2 * k, 2 * k - W + 1)

    pick_cols = jnp.where(row == nth(lane), 1.0, 0.0).astype(bf16)
    pick_rows = jnp.where(lane == nth(row), 1.0, 0.0).astype(bf16)

    def parts(x):
        for _ in range(3):
            part = x.astype(bf16)
            x = x - part.astype(f32)
            yield part

    x = sum(dot(part, pick_cols) for part in parts(meas[0, 0, m]))
    out[...] = sum(dot(pick_rows, part) for part in parts(x))


def spill_body(n, offs, above, *refs):
    m = lax.axis_index("mode")
    tx = lax.axis_index("tx")
    lane, row = iota(1), iota(0)
    total = jnp.zeros((W, W), f32)
    for k, slot in enumerate((m, 1 - m)[:n]):
        row0, q, s = place(offs, slot)
        total = total + jnp.where((q == 3) & (lane < s) & (row >= row0), refs[k][...], 0.0)
        row0, q, s = place(above, slot)
        keep = (q == 3) & (lane < s) & (row < row0) & (tx > 0)
        total = total + jnp.where(keep, refs[n + k][...], 0.0)
    refs[2 * n][...] = total


def take(out, ref, spot, rows):
    _, q, s = spot
    lane = iota(1)
    value = ref[...]
    here = pl.ds(pl.multiple_of(q * W, W), W)
    out[:, here] = out[:, here] - step_size * jnp.where(rows & (lane >= s), value, 0.0)
    nxt = pl.ds(pl.multiple_of(jnp.minimum(q + 1, 3) * W, W), W)
    keep = rows & (lane < s) & (q < 3)
    out[:, nxt] = out[:, nxt] - step_size * jnp.where(keep, value, 0.0)


def prior_body(c, filt, offs, obj, right, left, up, down, own, out):
    tx, ty = lax.axis_index("tx"), lax.axis_index("ty")
    n_tx, n_ty = lax.axis_size("tx"), lax.axis_size("ty")
    cols = obj.shape[2]
    shape = (W, cols)
    lane = lax.broadcasted_iota(jnp.int32, shape, 1)
    row = lax.broadcasted_iota(jnp.int32, shape, 0)
    taps = [[filt[i, k] for i in range(4)] for k in range(filt.shape[1])]
    g = [[sum(tap[i] * tap[j] for tap in taps) for j in range(4)] for i in range(4)]

    def beside(x, before, after):
        one_left = jnp.where(lane == 0, before, pltpu.roll(x, 1, 1))
        one_right = jnp.where(lane == cols - 1, after, pltpu.roll(x, cols - 1, 1))
        return one_left, one_right

    spot = place(offs, lax.axis_index("mode"))
    x = obj[c]
    after = jnp.where(ty == n_ty - 1, 0.0, right[:, 0:1])
    edge = jnp.broadcast_to(left[c : c + 1, :], (128, W)).T
    before = jnp.where(ty == 0, 0.0, edge[:, 0:1])

    def line(rim, flag, at):
        rim = jnp.where(flag, 0.0, rim)
        whole = jnp.concatenate([rim[k : k + 1, :] for k in range(4)], axis=1)
        return whole, rim[5:6, at : at + 1], rim[4:5, 0:1]

    u_mid, u_left, u_right = line(up[8 * c : 8 * c + 8, :], tx == 0, W - 1)
    d_mid, d_left, d_right = line(down[W + 8 * c : W + 8 * c + 8, :], tx == n_tx - 1, 0)
    xl, xr = beside(x, before, after)

    def over(mid, edge):
        return jnp.where(row == 0, edge, pltpu.roll(mid, 1, 0))

    def under(mid, edge):
        return jnp.where(row == W - 1, edge, pltpu.roll(mid, W - 1, 0))

    def shift_line(mid, b, a):
        l1 = lax.broadcasted_iota(jnp.int32, (1, cols), 1)
        return (
            jnp.where(l1 == 0, b, pltpu.roll(mid, 1, 1)),
            jnp.where(l1 == cols - 1, a, pltpu.roll(mid, cols - 1, 1)),
        )

    ul, ur = shift_line(u_mid, u_left, u_right)
    dl, dr = shift_line(d_mid, d_left, d_right)
    xu, xd = over(x, u_mid), under(x, d_mid)
    xul, xur = over(xl, ul), over(xr, ur)
    xdl, xdr = under(xl, dl), under(xr, dr)
    in_col = (lane > 0) | (ty > 0)
    in_row = (row > 0) | (tx > 0)
    total = g[0][0] * x + g[0][1] * xr + g[0][2] * xd + g[0][3] * xdr
    total += jnp.where(in_col, g[1][0] * xl + g[1][1] * x + g[1][2] * xdl + g[1][3] * xd, 0.0)
    total += jnp.where(in_row, g[2][0] * xu + g[2][1] * xur + g[2][2] * x + g[2][3] * xr, 0.0)
    total += jnp.where(
        in_row & in_col, g[3][0] * xul + g[3][1] * xu + g[3][2] * xl + g[3][3] * x, 0.0
    )
    out[...] = x - step_size * total
    take(out, own, spot, iota(0) >= spot[0])


def fold_body(offs, above, base, own_p, up_m, up_p, out):
    m = lax.axis_index("mode")
    row = iota(0)
    mine = place(offs, 1 - m)
    out[...] = base[...]
    take(out, own_p, mine, row >= mine[0])
    for ref, slot in ((up_m, m), (up_p, 1 - m)):
        over = place(above, slot)
        take(out, ref, over, (row < over[0]) & (lax.axis_index("tx") > 0))


def mid_body(offs, above, base, own_p, up_m, up_p, left_0, done, out, first):
    part = out.at[0]
    fold_body(offs, above, base, own_p, up_m, up_p, part)
    first[0] = part[:, 0:W] - step_size * jnp.where(lax.axis_index("ty") > 0, left_0[...], 0.0)
    out[1] = done[...]
    first[1] = done[:, 0:W]


def final_body(mid, first, left_0, left_1, out, buf, sems):
    ty = lax.axis_index("ty")
    stores = [pltpu.make_async_copy(buf.at[c], out.at[c, :, 0:W], sems.at[c]) for c in range(2)]
    for c, left in enumerate((left_0, left_1)):
        buf[c] = first[c] - step_size * jnp.where(ty > 0, left[...], 0.0)
        stores[c].start()
    for store in stores:
        store.wait()


def call(body, shapes, in_specs, limit, flops, bytes_accessed, scratch=(), out_spec=VMEM, aliases={}):
    many = isinstance(shapes, list)
    outs = [jax.ShapeDtypeStruct(s, f32) for s in (shapes if many else [shapes])]
    return pl.pallas_call(
        body,
        out_shape=outs if many else outs[0],
        in_specs=in_specs,
        out_specs=[out_spec] * len(outs) if many else out_spec,
        scratch_shapes=list(scratch),
        input_output_aliases=aliases,
        compiler_params=pltpu.CompilerParams(vmem_limit_bytes=limit << 20),
        cost_estimate=pl.CostEstimate(flops=flops, bytes_accessed=bytes_accessed, transcendentals=0),
    )


def local(ring, obj, probe, intensity, offsets, counts, filters):
    def go(value, where):
        return lax.ppermute(value, axes, ring[where])

    tabs = [jnp.asarray(t) for t in tables()]

    rows, cols = obj.shape[1:]
    piece = (W, W)
    whole = (2, rows, cols)
    offs = offsets.reshape(2, 2)
    right = [go(obj[0, :, :W], "left")]
    right.append(go(lax.optimization_barrier(obj)[1, :, :W], "left"))
    core = lax.rem(lax.axis_index("tx"), 2)
    probe_b = go(lax.dynamic_slice_in_dim(probe, core, 1, 0), "swap")
    probe_c = go(probe_b, "core")
    above = go(offs, "down")
    edge = call(edge_body, (8, W), [VMEM], 8, 1 << 16, 1 << 18)(obj)
    left = go(edge, "right")
    filt = filters.T
    meas = call(sort_body, piece, [VMEM], 8, 1 << 26, 3 << 18)(intensity)
    up_0 = call(
        functools.partial(send_body, 0), piece, [SMEM] + [VMEM] * 2, 8, 1 << 20, 2 << 20
    )(above, obj, right[0])
    below_0 = go(up_0, "up")
    up_1, rim = call(
        functools.partial(send_body, 1),
        [(W + 16, W), (16, W)],
        [SMEM] + [VMEM] * 4,
        8,
        1 << 20,
        2 << 20,
    )(above, obj, *right, left)
    below_1 = go(up_1, "up")
    over = go(rim, "down")
    g0, g1 = call(
        main_body,
        [piece] * 2,
        [SMEM, SMEM] + [VMEM] * 17,
        16,
        5 << 30,
        12 << 20,
        [pltpu.VMEM((4, 2, W, W), f32)],
    )(offs, counts, obj, *right, below_0, below_1, probe, probe_b, probe_c, meas, *tabs)
    p1, b0 = go(g1, "swap"), go(g0, "down")
    p0, b1 = go(g0, "swap"), go(g1, "down")
    base = [
        call(
            functools.partial(prior_body, c), (rows, cols), [SMEM] * 2 + [VMEM] * 6, 12, 1 << 27, 8 << 20
        )(filt, offs, obj, right[c], left, over, below_1, g)
        for c, g in ((0, g0), (1, g1))
    ]
    c1, c0 = go(p1, "down"), go(p0, "down")

    def spill(n, *args):
        specs = [SMEM, SMEM] + [VMEM] * (2 * n)
        kernel = call(functools.partial(spill_body, n), piece, specs, 8, 1 << 18, 1 << 20)
        return kernel(offs, above, *args)

    left_m0 = go(spill(1, g0, b0), "right")
    left_p0 = go(left_m0, "swap")
    left_1 = go(spill(2, g1, p1, b1, c1), "right")
    any_space = pl.BlockSpec(memory_space=pl.ANY)
    fold = call(fold_body, (rows, cols), [SMEM, SMEM] + [VMEM] * 4, 8, 1 << 20, 4 << 20)(
        offs, above, base[1], p1, b1, c1
    )
    mid, first = call(
        mid_body, [whole, (2, W, W)], [SMEM, SMEM] + [VMEM] * 6, 12, 1 << 24, 10 << 20
    )(offs, above, base[0], p0, b0, c0, left_m0, fold)
    return call(
        final_body,
        whole,
        [any_space] + [VMEM] * 3,
        8,
        1 << 18,
        2 << 20,
        [pltpu.VMEM((2, W, W), f32), pltpu.SemaphoreType.DMA((2,))],
        any_space,
        {0: 0},
    )(mid, first, left_p0, left_1)


def solution(mesh):
    placed = (
        P(None, "tx", "ty"),
        P("mode", None, None, None),
        P("tx", "ty", None, None, None),
        P("tx", "ty", None, None),
        P("tx", "ty"),
        P(),
    )

    def body(*args):
        return local(rings(mesh), *args)

    return jax.shard_map(
        body, mesh=mesh, in_specs=placed, out_specs=P(None, "tx", "ty"), check_vma=False
    )
```
